32 devices in a mesh: parts: 1, ctx: 32 (over z, y, x, core).
Axes of the slice: x: 2, y: 2, z: 4, core: 2. Of those that a mesh axis runs over, the one named last changes fastest.
Arguments:
- query_rows: bfloat16 [8192, 512], P(('parts', 'ctx')), may hold values from -6 to 6
- key_rows: bfloat16 [8192, 512], P(('parts', 'ctx')), may hold values from -6 to 6
- value_rows: bfloat16 [8192, 512], P(('parts', 'ctx')), may hold values from -6 to 6
- grad_out: bfloat16 [8192, 512], P(('parts', 'ctx')), may hold values from -6 to 6
- stripe_lists: int32 [64, 16], P(('parts', 'ctx')), may hold values from 0 to 31, all different within a row
Outputs:
- grad_query: float32 [8192, 512], P(('parts', 'ctx'))
- grad_key: float32 [8192, 512], P(('parts', 'ctx'))
- grad_value: float32 [8192, 512], P(('parts', 'ctx'))
The draws below stay inside these ranges and needn't reach their ends.
Inputs may be any that keep to these rules, and one draw needn't show every extreme that they name: `stripe_lists`: the 16 shards listed for one query block are distinct.
All inputs are finite; a program needn't handle non-finite values.
Results may differ from the reference program's by a relative error of at most 0.012.
Values may be sent and summed in bfloat16 or wider, within the bound.
No kernel may reach another device: no remote copies, remote signals or barrier semaphores. Data moves between devices by JAX's collectives and lax.ppermute only.
A program may use at most 64 MiB of HBM per device.

```python
import jax
import jax.numpy as jnp
from jax import lax

HEADS = 8
HEAD_DIM = 64
WIDTH = 512
BLOCK = 128
WIN = 2
STRIPE = 16
NCOL = 16
TOK_DEV = 256
LENGTH = 8192
NBLOCKS = 64
N_CTX = 32


def draw_pair(key):
    first_key = jax.random.fold_in(key, 11)
    second_key = jax.random.fold_in(key, 12)
    query_base = jnp.clip(jax.random.normal(first_key, (LENGTH, WIDTH), jnp.float32), -4.0, 4.0)
    key_base = jnp.clip(jax.random.normal(second_key, (LENGTH, WIDTH), jnp.float32), -4.0, 4.0)
    return (query_base.astype(jnp.bfloat16), key_base.astype(jnp.bfloat16))


def draw_query_rows(key, part):
    return draw_pair(key)[0]


def draw_key_rows(key, part):
    return draw_pair(key)[1]


def levels(own_key, shape, split, least, top_value):
    loudness = 1.0
    for axis_at, parts in split:
        heights = jax.random.uniform(jax.random.fold_in(jax.random.fold_in(own_key, 6), axis_at), (parts,), jnp.float32, least / len(split), top_value / len(split))
        loudness = loudness * jnp.repeat(jnp.exp(heights), shape[axis_at] // parts).reshape((-1,) + (1,) * (len(shape) - 1 - axis_at))
    return loudness


def picks_of(stream_key, rows, amount, top, lift):
    sequence = jax.random.permutation(jax.random.fold_in(stream_key, 1), amount)
    favour = sequence
    for power in range(3):
        favour = favour * favour // amount
    favour = favour * lift // amount
    chance = jax.random.randint(jax.random.fold_in(stream_key, 2), (rows, amount), 0, 4096) + favour
    fixed_rows = jax.random.permutation(jax.random.fold_in(stream_key, 3), rows)[jnp.arange(amount) % rows]
    chance = jnp.where(jnp.arange(rows)[:, None] == fixed_rows[None, :], 1 << 14, chance)
    priority = chance * amount + jnp.arange(amount)
    return lax.top_k(priority.astype(jnp.int32), top)[1].astype(jnp.int32)


def normal_values(key, extent, scale, reach, cuts=(), kind=jnp.bfloat16):
    result = scale * jax.random.normal(key, extent, jnp.float32)
    if cuts:
        result = result * levels(key, extent, cuts, -0.22, 0.18)
    return jnp.clip(result, -reach, reach).astype(kind)


def setup_inputs(seed: int = 0, part: int = 0) -> dict:
    key_list = jax.random.split(jax.random.key(seed), 6)
    part_keys = jax.random.split(jax.random.fold_in(key_list[5], part), 6)
    return {
        "query_rows": draw_query_rows(jax.random.fold_in(jax.random.fold_in(key_list[5], part), 71), part),
        "key_rows": draw_key_rows(jax.random.fold_in(jax.random.fold_in(key_list[5], part), 71), part),
        "value_rows": normal_values(part_keys[2], (LENGTH, WIDTH), 1.0, 6.0, ((0, 32),)),
        "grad_out": normal_values(part_keys[3], (LENGTH, WIDTH), 1.0, 6.0, ((0, 32),)),
        "stripe_lists": picks_of(part_keys[4], NBLOCKS, N_CTX, NCOL, 0),
    }


def block_gradients(query_block, key_block, value_block, grad_block, key_valid):
    score_scale = HEAD_DIM ** -0.5
    query_three = query_block.astype(jnp.float32).reshape(-1, HEADS, HEAD_DIM)
    key_three = key_block.astype(jnp.float32).reshape(-1, HEADS, HEAD_DIM)
    value_three = value_block.astype(jnp.float32).reshape(-1, HEADS, HEAD_DIM)
    grad_three = grad_block.astype(jnp.float32).reshape(-1, HEADS, HEAD_DIM)
    scores = jnp.einsum("qhd,khd->hqk", query_three, key_three) * score_scale
    scores = jnp.where(key_valid[None, None, :], scores, -jnp.inf)
    maxima = jnp.max(scores, axis=-1, keepdims=True)
    raised = jnp.exp(scores - maxima)
    weights = raised / jnp.sum(raised, axis=-1, keepdims=True)
    weights_low = weights.astype(jnp.bfloat16).astype(jnp.float32)
    attended = jnp.einsum("hqk,khd->qhd", weights_low, value_three)
    row_dot = jnp.transpose(jnp.sum(grad_three * attended, axis=-1))
    grad_weights = jnp.einsum("qhd,khd->hqk", grad_three, value_three)
    grad_scores = (weights * (grad_weights - row_dot[:, :, None]) * score_scale).astype(jnp.bfloat16).astype(jnp.float32)
    grad_query = jnp.einsum("hqk,khd->qhd", grad_scores, key_three)
    grad_key = jnp.einsum("hqk,qhd->khd", grad_scores, query_three)
    grad_value = jnp.einsum("hqk,qhd->khd", weights_low, grad_three)
    return grad_query.reshape(-1, WIDTH), grad_key.reshape(-1, WIDTH), grad_value.reshape(-1, WIDTH)


def reference(query_rows, key_rows, value_rows, grad_out, stripe_lists):
    halo_rows = WIN * BLOCK
    window_rows = (2 * WIN + 1) * BLOCK
    key_padded = jnp.pad(key_rows, ((halo_rows, halo_rows), (0, 0)))
    value_padded = jnp.pad(value_rows, ((halo_rows, halo_rows), (0, 0)))
    key_stripes = key_rows.reshape(N_CTX, TOK_DEV, WIDTH)[:, TOK_DEV - STRIPE:, :]
    value_stripes = value_rows.reshape(N_CTX, TOK_DEV, WIDTH)[:, TOK_DEV - STRIPE:, :]

    def block_step(carry, block_id):
        key_sums, value_sums, key_table, value_table = carry
        start_row = block_id * BLOCK
        query_block = lax.dynamic_slice_in_dim(query_rows, start_row, BLOCK, 0)
        grad_block = lax.dynamic_slice_in_dim(grad_out, start_row, BLOCK, 0)
        near_keys = lax.dynamic_slice_in_dim(key_padded, start_row, window_rows, 0)
        near_values = lax.dynamic_slice_in_dim(value_padded, start_row, window_rows, 0)
        chosen = stripe_lists[block_id]
        far_keys = key_stripes[chosen].reshape(NCOL * STRIPE, WIDTH)
        far_values = value_stripes[chosen].reshape(NCOL * STRIPE, WIDTH)
        window_ids = block_id - WIN + jnp.arange(2 * WIN + 1, dtype=jnp.int32)
        block_valid = (window_ids >= 0) & (window_ids < NBLOCKS)
        key_valid = jnp.concatenate([jnp.repeat(block_valid, BLOCK), jnp.ones((NCOL * STRIPE,), bool)])
        grad_query, grad_key, grad_value = block_gradients(
            query_block,
            jnp.concatenate([near_keys, far_keys], axis=0),
            jnp.concatenate([near_values, far_values], axis=0),
            grad_block,
            key_valid,
        )
        key_sums = lax.dynamic_update_slice_in_dim(
            key_sums, lax.dynamic_slice_in_dim(key_sums, start_row, window_rows, 0) + grad_key[:window_rows], start_row, 0)
        value_sums = lax.dynamic_update_slice_in_dim(
            value_sums, lax.dynamic_slice_in_dim(value_sums, start_row, window_rows, 0) + grad_value[:window_rows], start_row, 0)
        key_table = key_table.at[chosen].add(grad_key[window_rows:].reshape(NCOL, STRIPE, WIDTH))
        value_table = value_table.at[chosen].add(grad_value[window_rows:].reshape(NCOL, STRIPE, WIDTH))
        return (key_sums, value_sums, key_table, value_table), grad_query

    init = (
        jnp.zeros((LENGTH + 2 * halo_rows, WIDTH), jnp.float32),
        jnp.zeros((LENGTH + 2 * halo_rows, WIDTH), jnp.float32),
        jnp.zeros((N_CTX, STRIPE, WIDTH), jnp.float32),
        jnp.zeros((N_CTX, STRIPE, WIDTH), jnp.float32),
    )
    (key_sums, value_sums, key_table, value_table), query_parts = lax.scan(
        block_step, init, jnp.arange(NBLOCKS, dtype=jnp.int32))
    key_sums = key_sums[halo_rows:halo_rows + LENGTH].reshape(N_CTX, TOK_DEV, WIDTH)
    value_sums = value_sums[halo_rows:halo_rows + LENGTH].reshape(N_CTX, TOK_DEV, WIDTH)
    key_sums = key_sums.at[:, TOK_DEV - STRIPE:, :].add(key_table).reshape(LENGTH, WIDTH)
    value_sums = value_sums.at[:, TOK_DEV - STRIPE:, :].add(value_table).reshape(LENGTH, WIDTH)
    return query_parts.reshape(LENGTH, WIDTH), key_sums, value_sums
```

```python
import functools

import jax
import jax.numpy as jnp
from jax import lax
from jax.experimental import pallas as pl
from jax.experimental.pallas import tpu as pltpu
from jax.sharding import PartitionSpec as P

HEAD_DIM = 64
BLOCK = 128
WIN = 2
STRIPE = 16
NCOL = 16
LANES = 128
ROWS = 2 * BLOCK
EXT = 3 * ROWS
FAR = NCOL * STRIPE
SPAN = (2 * WIN + 1) * BLOCK
SCALE = HEAD_DIM**-0.5
NT = (((1,), (1,)), ((), ()))


def attention_kernel(
    slots, flags, biases, query, grad, own, mate, across, table_a, table_b,
    grad_query, grad_own, grad_mate, grad_across, table_keep, table_send,
    ext_k, ext_v, table, far_k, far_v, q_two, g_two, probs, scores, far_probs, far_scores,
    ext_sum, table_sum,
):
    half = table_a.shape[0]
    mate_at = pl.multiple_of(flags[0], ROWS)
    across_at = pl.multiple_of(flags[1], ROWS)
    for which, ext in ((0, ext_k), (1, ext_v)):
        ext[ROWS : 2 * ROWS] = own[which]
        ext[pl.ds(mate_at, ROWS)] = mate[which]
        ext[pl.ds(across_at, ROWS)] = across[which]
    table[:half] = table_a[...]
    table[half:] = table_b[...]
    for i in range(2):
        for j in range(NCOL):
            slot = slots[i, j]
            far_k[i, j * STRIPE : (j + 1) * STRIPE] = table[slot, 0]
            far_v[i, j * STRIPE : (j + 1) * STRIPE] = table[slot, 1]
    first = lax.broadcasted_iota(jnp.int32, (ROWS, LANES), 1) < HEAD_DIM
    q = query[...] * jnp.bfloat16(SCALE)
    g = grad[...]
    zero = jnp.zeros_like(q)
    q_two[:ROWS] = jnp.where(first, q, zero)
    q_two[ROWS:] = jnp.where(first, zero, q)
    g_two[:ROWS] = jnp.where(first, g, zero)
    g_two[ROWS:] = jnp.where(first, zero, g)

    @pl.when(pl.program_id(0) == 0)
    def _():
        probs[...] = jnp.zeros_like(probs)
        scores[...] = jnp.zeros_like(scores)

    for h in range(2):
        qh = q_two[h * ROWS : (h + 1) * ROWS]
        gh = g_two[h * ROWS : (h + 1) * ROWS]
        s_win = lax.dot_general(ext_k[...], qh, NT, preferred_element_type=jnp.float32)
        d_win = lax.dot_general(ext_v[...], gh, NT, preferred_element_type=jnp.float32)
        for i in range(2):
            rows = slice(i * BLOCK, i * BLOCK + SPAN)
            cols = slice(i * BLOCK, (i + 1) * BLOCK)
            qi, gi = qh[cols], gh[cols]
            s_far = lax.dot_general(far_k[i], qi, NT, preferred_element_type=jnp.float32)
            d_far = lax.dot_general(far_v[i], gi, NT, preferred_element_type=jnp.float32)
            edge = ROWS - i * BLOCK
            s = s_win[rows, cols]
            s = jnp.concatenate(
                [s[:edge] + biases[0], s[edge : edge + ROWS], s[edge + ROWS :] + biases[1]], axis=0
            )
            d = d_win[rows, cols]
            top = jnp.maximum(
                jnp.max(s, axis=0, keepdims=True), jnp.max(s_far, axis=0, keepdims=True)
            )
            u = jnp.exp(s - top)
            u_far = jnp.exp(s_far - top)
            total = jnp.sum(u, axis=0, keepdims=True) + jnp.sum(u_far, axis=0, keepdims=True)
            inv = 1.0 / total
            dot = jnp.sum(u * d, axis=0, keepdims=True) + jnp.sum(u_far * d_far, axis=0, keepdims=True)
            dot = dot * inv
            p = u * inv
            p_far = u_far * inv
            wide = slice(h * ROWS + i * BLOCK, h * ROWS + (i + 1) * BLOCK)
            narrow = slice(h * BLOCK, (h + 1) * BLOCK)
            probs[rows, wide] = p.astype(jnp.bfloat16)
            scores[rows, wide] = (p * (d - dot)).astype(jnp.bfloat16)
            far_probs[i, :, narrow] = p_far.astype(jnp.bfloat16)
            far_scores[i, :, narrow] = (p_far * (d_far - dot)).astype(jnp.bfloat16)

    table_sum[...] = jnp.zeros_like(table_sum)
    for which, left, left_far, right in (
        (0, scores, far_scores, q_two),
        (1, probs, far_probs, g_two),
    ):
        ext_sum[which] = jnp.dot(left[...], right[...], preferred_element_type=jnp.float32)
        for i in range(2):
            cols = slice(i * BLOCK, (i + 1) * BLOCK)
            both = jnp.concatenate(
                [right[i * BLOCK : (i + 1) * BLOCK], right[ROWS + i * BLOCK : ROWS + (i + 1) * BLOCK]],
                axis=0,
            )
            far = jnp.dot(left_far[i], both, preferred_element_type=jnp.float32)
            for j in range(NCOL):
                slot = slots[i, j]
                table_sum[slot, which] += far[j * STRIPE : (j + 1) * STRIPE]
        grad_own[which] = ext_sum[which, ROWS : 2 * ROWS]
        grad_mate[which] = ext_sum[which, pl.ds(mate_at, ROWS)].astype(grad_mate.dtype)
        grad_across[which] = ext_sum[which, pl.ds(across_at, ROWS)].astype(grad_across.dtype)
    table_keep[...] = table_sum[:half]
    table_send[...] = table_sum[half:].astype(table_send.dtype)

    k_t = jnp.transpose(ext_k[...])
    f_t = [jnp.transpose(far_k[i]) for i in range(2)]
    parts = []
    for h in range(2):
        feats = slice(h * HEAD_DIM, (h + 1) * HEAD_DIM)
        near = jnp.dot(
            k_t[feats], scores[:, h * ROWS : (h + 1) * ROWS], preferred_element_type=jnp.float32
        )
        far = [
            jnp.dot(
                f_t[i][feats],
                far_scores[i, :, h * BLOCK : (h + 1) * BLOCK],
                preferred_element_type=jnp.float32,
            )
            for i in range(2)
        ]
        parts.append(near + jnp.concatenate(far, axis=1))
    grad_query[...] = jnp.transpose(jnp.concatenate(parts, axis=0)) * SCALE


def attention(slots, flags, biases, query, grad, own, mate, across, table_a, table_b):
    half = table_a.shape[0]
    width = query.shape[1]
    steps = width // LANES
    rows = pl.BlockSpec((ROWS, LANES), lambda p: (0, p))
    pair = pl.BlockSpec((2, ROWS, LANES), lambda p: (0, 0, p))
    tab = pl.BlockSpec((half, 2, STRIPE, LANES), lambda p: (0, 0, 0, p))
    smem = pl.BlockSpec(memory_space=pltpu.SMEM)
    bf16, f32 = jnp.bfloat16, jnp.float32
    return pl.pallas_call(
        attention_kernel,
        grid=(steps,),
        in_specs=[smem, smem, smem, rows, rows, pair, pair, pair, tab, tab],
        out_specs=[rows, pair, pair, pair, tab, tab],
        out_shape=[
            jax.ShapeDtypeStruct((ROWS, width), f32),
            jax.ShapeDtypeStruct((2, ROWS, width), f32),
            jax.ShapeDtypeStruct((2, ROWS, width), bf16),
            jax.ShapeDtypeStruct((2, ROWS, width), bf16),
            jax.ShapeDtypeStruct((half, 2, STRIPE, width), f32),
            jax.ShapeDtypeStruct((half, 2, STRIPE, width), bf16),
        ],
        scratch_shapes=[
            pltpu.VMEM((EXT, LANES), bf16),
            pltpu.VMEM((EXT, LANES), bf16),
            pltpu.VMEM((2 * half, 2, STRIPE, LANES), bf16),
            pltpu.VMEM((2, FAR, LANES), bf16),
            pltpu.VMEM((2, FAR, LANES), bf16),
            pltpu.VMEM((2 * ROWS, LANES), bf16),
            pltpu.VMEM((2 * ROWS, LANES), bf16),
            pltpu.VMEM((EXT, 2 * ROWS), bf16),
            pltpu.VMEM((EXT, 2 * ROWS), bf16),
            pltpu.VMEM((2, FAR, 2 * BLOCK), bf16),
            pltpu.VMEM((2, FAR, 2 * BLOCK), bf16),
            pltpu.VMEM((2, EXT, LANES), f32),
            pltpu.VMEM((2 * half, 2, STRIPE, LANES), f32),
        ],
        compiler_params=pltpu.CompilerParams(vmem_limit_bytes=48 << 20),
        cost_estimate=pl.CostEstimate(flops=3_000_000_000, bytes_accessed=8 << 20, transcendentals=1 << 21),
    )(slots, flags, biases, query, grad, own, mate, across, table_a, table_b)


def stage_bits(count):
    if count == 32:
        return [8, 16, 2, 4, 1]
    bits = [1 << k for k in range(count.bit_length() - 1)]
    return bits[1:] + bits[:1]


def swapped(x, count, bit):
    return lax.ppermute(x, "ctx", [(i, i ^ bit) for i in range(count)])


def crossed(x, count):
    up = [(i, i + 1) for i in range(1, count - 1, 2)]
    return lax.ppermute(x, "ctx", up + [(j, i) for i, j in up])


def body(query_rows, key_rows, value_rows, grad_out, stripe_lists):
    count = lax.axis_size("ctx")
    me = lax.axis_index("ctx")
    bits = stage_bits(count)
    own = jnp.stack([key_rows, value_rows])
    across = crossed(own, count)
    mate = swapped(own, count, 1)
    gathered = own[None, :, ROWS - STRIPE :]
    for bit in bits[:-1]:
        gathered = jnp.concatenate([gathered, swapped(gathered, count, bit)], axis=0)
    other = swapped(gathered, count, bits[-1])

    relative = stripe_lists ^ me
    slots = jnp.zeros_like(relative)
    for place, bit in enumerate(bits):
        slots = slots | jnp.where((relative & bit) != 0, 1 << place, 0)
    odd = me % 2
    flags = jnp.stack([jnp.where(odd, 0, 2 * ROWS), jnp.where(odd, 2 * ROWS, 0)]).astype(jnp.int32)
    biases = jnp.stack(
        [jnp.where(me == 0, -jnp.inf, 0.0), jnp.where(me == count - 1, -jnp.inf, 0.0)]
    ).astype(jnp.float32)
    grad_query, grad_own, grad_mate, grad_across, keep, send = attention(
        slots, flags, biases, query_rows, grad_out, own, mate, across, gathered, other
    )
    from_across = crossed(grad_across, count)
    from_mate = swapped(grad_mate, count, 1)
    for bit in bits[::-1]:
        total = keep + swapped(send, count, bit).astype(jnp.float32)
        half = total.shape[0] // 2
        keep, send = total[:half], total[half:].astype(jnp.bfloat16)
    tail = jnp.pad(total[0], ((0, 0), (ROWS - STRIPE, 0), (0, 0)))
    owned = grad_own + from_mate.astype(jnp.float32) + from_across.astype(jnp.float32) + tail
    return grad_query, owned[0], owned[1]


def solution(mesh):
    spec = P(("parts", "ctx"), None)
    return jax.shard_map(
        body,
        mesh=mesh,
        in_specs=(spec,) * 5,
        out_specs=(spec,) * 3,
        check_vma=False,
    )
```

```python
import jax
import jax.numpy as jnp
from jax import lax
from jax.experimental import pallas as pl
from jax.experimental.pallas import tpu as pltpu
from jax.sharding import PartitionSpec as P

HEAD_DIM = 64
BLOCK = 128
WIN = 2
STRIPE = 16
NCOL = 16
LANES = 128
ROWS = WIN * BLOCK
EXT = 3 * ROWS
FAR = NCOL * STRIPE
SPAN = (2 * WIN + 1) * BLOCK
SCALE = HEAD_DIM**-0.5
NT = (((1,), (1,)), ((), ()))
BF16, F32 = jnp.bfloat16, jnp.float32


def tile(h, i):
    return slice((2 * h + i) * BLOCK, (2 * h + i + 1) * BLOCK)


def block_rows(i, flip):
    return pl.ds(pl.multiple_of((i ^ flip) * BLOCK, BLOCK), BLOCK)


def split_heads(ref, which, flip, two):
    first = lax.broadcasted_iota(jnp.int32, (BLOCK, LANES), 1) < HEAD_DIM
    for i in range(2):
        x = ref[which, block_rows(i, flip)]
        zero = jnp.zeros_like(x)
        two[tile(0, i)] = jnp.where(first, x, zero)
        two[tile(1, i)] = jnp.where(first, zero, x)


def fill_window(flip, mate, own, which, across, ext):
    for i in range(2):
        rows = block_rows(i, flip)
        ext[tile(0, i)] = mate[rows]
        ext[tile(1, i)] = own[which, rows]
        ext[tile(2, i)] = across[rows]


def column_max(x):
    return jnp.max(x, axis=0, keepdims=True)


def column_sum(x):
    return jnp.sum(x, axis=0, keepdims=True)


def near_rows(i):
    return slice(i * BLOCK, i * BLOCK + SPAN)


def window_kernel(
    flags, biases, pair, own, mate_k, across_k, mate_v, across_v,
    near_s, near_d, stats,
    ext_k, ext_v, q_two, g_two,
):
    flip = flags[0]
    fill_window(flip, mate_k, own, 0, across_k, ext_k)
    fill_window(flip, mate_v, own, 1, across_v, ext_v)
    split_heads(pair, 0, flip, q_two)
    split_heads(pair, 1, flip, g_two)
    for h in range(2):
        heads = slice(h * ROWS, (h + 1) * ROWS)
        s = lax.dot_general(ext_k[...], q_two[heads], NT, preferred_element_type=F32)
        near_s[0, : 2 * ROWS, heads] = s[: 2 * ROWS]
        near_s[0, 2 * ROWS :, heads] = s[2 * ROWS :] + biases[0]
        near_d[0, :, heads] = lax.dot_general(
            ext_v[...], g_two[heads], NT, preferred_element_type=F32
        )
    for h in range(2):
        for i in range(2):
            s = near_s[0, near_rows(i), tile(h, i)]
            d = near_d[0, near_rows(i), tile(h, i)]
            top = column_max(s)
            u = jnp.exp(s - top)
            stats[0, 0:1, tile(h, i)] = top
            stats[0, 1:2, tile(h, i)] = column_sum(u)
            stats[0, 2:3, tile(h, i)] = column_sum(u * d)


def stripe_kernel(
    flags, slots, pair, stats, table_a, table_b, coefs, far_query, table_keep, table_send,
    table, far_k, far_v, q_two, g_two, far_probs, far_scores, table_sum,
):
    flip = flags[0]
    half = table_a.shape[0]
    table[:half] = table_a[...]
    table[half:] = table_b[...]
    for i in range(2):
        for j in range(NCOL):
            slot = slots[i ^ flip, j]
            far_k[i, j * STRIPE : (j + 1) * STRIPE] = table[slot, 0]
            far_v[i, j * STRIPE : (j + 1) * STRIPE] = table[slot, 1]
    split_heads(pair, 0, flip, q_two)
    split_heads(pair, 1, flip, g_two)
    tiles = [(h, i) for h in range(2) for i in range(2)]
    s = jnp.concatenate(
        [
            lax.dot_general(far_k[i], q_two[tile(h, i)], NT, preferred_element_type=F32)
            for h, i in tiles
        ],
        axis=1,
    )
    d = jnp.concatenate(
        [
            lax.dot_general(far_v[i], g_two[tile(h, i)], NT, preferred_element_type=F32)
            for h, i in tiles
        ],
        axis=1,
    )
    near_top = stats[0, 0:1]
    top = jnp.maximum(near_top, column_max(s))
    shrink = jnp.exp(near_top - top)
    u = jnp.exp(s - top)
    total = stats[0, 1:2] * shrink + column_sum(u)
    inv = 1.0 / total
    dot = (stats[0, 2:3] * shrink + column_sum(u * d)) * inv
    coefs[0, 0:1] = top + jnp.log(total)
    coefs[0, 1:2] = dot
    p = u * inv
    far_probs[...] = p.astype(BF16)
    far_scores[...] = (p * (d - dot)).astype(BF16)
    table_sum[...] = jnp.zeros_like(table_sum)
    for which, left, right in ((0, far_scores, q_two), (1, far_probs, g_two)):
        for i in range(2):
            far = jnp.dot(
                jnp.concatenate([left[:, tile(0, i)], left[:, tile(1, i)]], axis=1),
                jnp.concatenate([right[tile(0, i)], right[tile(1, i)]], axis=0),
                preferred_element_type=F32,
            )
            for j in range(NCOL):
                slot = slots[i ^ flip, j]
                table_sum[slot, which] += far[j * STRIPE : (j + 1) * STRIPE]
    table_keep[...] = table_sum[:half]
    table_send[...] = table_sum[half:].astype(table_send.dtype)
    for i in range(2):
        k_t = jnp.transpose(far_k[i])
        for h in range(2):
            feats = slice(h * HEAD_DIM, (h + 1) * HEAD_DIM)
            far_query[0, feats, i * BLOCK : (i + 1) * BLOCK] = jnp.dot(
                k_t[feats], far_scores[:, tile(h, i)], preferred_element_type=F32
            )


def gradient_kernel(
    flags, pair, own, mate_k, across_k, near_s, near_d, coefs, far_query,
    grad_query, grad_key, grad_value, grad_mate, grad_across,
    ext_k, q_two, g_two, probs, scores,
):
    flip = flags[0]
    fill_window(flip, mate_k, own, 0, across_k, ext_k)
    split_heads(pair, 0, flip, q_two)
    split_heads(pair, 1, flip, g_two)

    for h in range(2):
        for i in range(2):
            idle = slice((1 - i) * SPAN, (1 - i) * SPAN + BLOCK)
            probs[idle, tile(h, i)] = jnp.zeros((BLOCK, BLOCK), BF16)
            scores[idle, tile(h, i)] = jnp.zeros((BLOCK, BLOCK), BF16)

    for h in range(2):
        for i in range(2):
            rows = near_rows(i)
            p = jnp.exp(near_s[0, rows, tile(h, i)] - coefs[0, 0:1, tile(h, i)])
            probs[rows, tile(h, i)] = p.astype(BF16)
            ds = p * (near_d[0, rows, tile(h, i)] - coefs[0, 1:2, tile(h, i)])
            scores[rows, tile(h, i)] = ds.astype(BF16)
    for which, left, right, grad_own in (
        (0, scores, q_two, grad_key),
        (1, probs, g_two, grad_value),
    ):
        total = jnp.dot(left[...], right[...], preferred_element_type=F32)
        for i in range(2):
            rows = block_rows(i, flip)
            grad_mate[which, rows] = total[tile(0, i)].astype(grad_mate.dtype)
            grad_own[rows] = total[tile(1, i)]
            grad_across[which, rows] = total[tile(2, i)].astype(grad_across.dtype)
    k_t = jnp.transpose(ext_k[...])
    near = [
        jnp.dot(
            k_t[h * HEAD_DIM : (h + 1) * HEAD_DIM],
            scores[:, h * ROWS : (h + 1) * ROWS],
            preferred_element_type=F32,
        )
        for h in range(2)
    ]
    out = jnp.transpose(jnp.concatenate(near, axis=0) + far_query[0]) * SCALE
    for i in range(2):
        grad_query[block_rows(i, flip)] = out[i * BLOCK : (i + 1) * BLOCK]


SMEM_SPEC = pl.BlockSpec(memory_space=pltpu.SMEM)
VMEM_SPEC = pl.BlockSpec(memory_space=pltpu.VMEM)
TWO = pltpu.VMEM((2 * ROWS, LANES), BF16)
EXTENT = pltpu.VMEM((EXT, LANES), BF16)
FULL, ROW, PAIR, TABLE, STEP = "full", "row", "pair", "table", "step"


def view(ref, kind, p):
    lanes = pl.ds(p * LANES, LANES)
    if kind == ROW:
        return ref.at[:, lanes]
    if kind == PAIR:
        return ref.at[:, :, lanes]
    if kind == TABLE:
        return ref.at[:, :, :, lanes]
    if kind == STEP:
        return ref.at[pl.ds(p, 1)]
    return ref


def call(kernel, steps, in_kinds, out_kinds, out_shape, scratch, flops, moved, args):
    kinds = in_kinds + out_kinds

    def whole(*refs):
        for p in range(steps):
            views = [view(ref, kind, p) for ref, kind in zip(refs, kinds)]
            kernel(*views, *refs[len(kinds) :])

    return pl.pallas_call(
        whole,
        in_specs=[SMEM_SPEC if kind == FULL else VMEM_SPEC for kind in in_kinds],
        out_specs=[VMEM_SPEC] * len(out_kinds),
        out_shape=[jax.ShapeDtypeStruct(shape, dtype) for shape, dtype in out_shape],
        scratch_shapes=scratch,
        compiler_params=pltpu.CompilerParams(vmem_limit_bytes=24 << 20),
        cost_estimate=pl.CostEstimate(flops=flops, bytes_accessed=moved, transcendentals=1 << 20),
    )(*args)


def window_part(flags, biases, pair, own, mate_k, across_k, mate_v, across_v):
    steps = pair.shape[2] // LANES
    near = ((steps, EXT, 2 * ROWS), F32)
    return call(
        window_kernel,
        steps,
        [FULL, FULL, PAIR, PAIR, ROW, ROW, ROW, ROW],
        [STEP, STEP, STEP],
        [near, near, ((steps, 8, 2 * ROWS), F32)],
        [EXTENT, EXTENT, TWO, TWO],
        1 << 34,
        12 << 20,
        (flags, biases, pair, own, mate_k, across_k, mate_v, across_v),
    )


def stripe_part(flags, slots, pair, stats, table_a, table_b):
    half = table_a.shape[0]
    width = pair.shape[2]
    steps = width // LANES
    return call(
        stripe_kernel,
        steps,
        [FULL, FULL, PAIR, STEP, TABLE, TABLE],
        [STEP, STEP, TABLE, TABLE],
        [
            ((steps, 8, 2 * ROWS), F32),
            ((steps, LANES, ROWS), F32),
            ((half, 2, STRIPE, width), F32),
            ((half, 2, STRIPE, width), BF16),
        ],
        [
            pltpu.VMEM((2 * half, 2, STRIPE, LANES), BF16),
            pltpu.VMEM((2, FAR, LANES), BF16),
            pltpu.VMEM((2, FAR, LANES), BF16),
            TWO,
            TWO,
            pltpu.VMEM((FAR, 4 * BLOCK), BF16),
            pltpu.VMEM((FAR, 4 * BLOCK), BF16),
            pltpu.VMEM((2 * half, 2, STRIPE, LANES), F32),
        ],
        1 << 30,
        4 << 20,
        (flags, slots, pair, stats, table_a, table_b),
    )


def gradient_part(flags, pair, own, mate_k, across_k, near_s, near_d, coefs, far_query):
    width = pair.shape[2]
    steps = width // LANES
    return call(
        gradient_kernel,
        steps,
        [FULL, PAIR, PAIR, ROW, ROW, STEP, STEP, STEP, STEP],
        [ROW, ROW, ROW, PAIR, PAIR],
        [((ROWS, width), F32)] * 3 + [((2, ROWS, width), BF16)] * 2,
        [
            EXTENT,
            TWO,
            TWO,
            pltpu.VMEM((EXT, 2 * ROWS), BF16),
            pltpu.VMEM((EXT, 2 * ROWS), BF16),
        ],
        1 << 34,
        14 << 20,
        (flags, pair, own, mate_k, across_k, near_s, near_d, coefs, far_query),
    )


def stage_bits(count):
    if count == 32:
        return [8, 16, 4, 2, 1]
    bits = [1 << k for k in range(count.bit_length() - 1)]
    return bits[1:] + bits[:1]


def swapped(x, count, bit):
    return lax.ppermute(x, "ctx", [(i, i ^ bit) for i in range(count)])


def crossed(x, count):
    up = [(i, i + 1) for i in range(1, count - 1, 2)]
    return lax.ppermute(x, "ctx", up + [(j, i) for i, j in up])


def body(query_rows, key_rows, value_rows, grad_out, stripe_lists):
    count = lax.axis_size("ctx")
    me = lax.axis_index("ctx")
    bits = stage_bits(count)
    x_bit, y_bit = bits[-2], bits[-3]
    relative = stripe_lists ^ me
    slots = jnp.zeros_like(relative)
    for place, bit in enumerate(bits):
        slots = slots | jnp.where((relative & bit) != 0, 1 << place, 0)
    flags = (1 - (me & 1)).reshape(1)
    alone = (me == 0) | (me == count - 1)
    biases = jnp.where(alone, -jnp.inf, 0.0).astype(F32).reshape(1)

    pair = jnp.stack([query_rows * BF16(SCALE), grad_out])
    own = jnp.stack([key_rows, value_rows])
    across_k = crossed(key_rows, count)
    across_v = crossed(value_rows, count)
    mate_k = swapped(key_rows, count, 1)
    mate_v = swapped(value_rows, count, 1)
    gathered = jnp.stack([key_rows[ROWS - STRIPE :], value_rows[ROWS - STRIPE :]])[None]
    for bit in bits[:-1]:
        if bit == y_bit:
            gathered, across_k = lax.optimization_barrier((gathered, across_k))
        if bit == x_bit:
            gathered, across_v, mate_k, mate_v = lax.optimization_barrier(
                (gathered, across_v, mate_k, mate_v)
            )
            near_s, near_d, stats = window_part(
                flags, biases, pair, own, mate_k, across_k, mate_v, across_v
            )
        gathered = jnp.concatenate([gathered, swapped(gathered, count, bit)], axis=0)
    gathered, stats = lax.optimization_barrier((gathered, stats))
    other = swapped(gathered, count, bits[-1])
    coefs, far_query, keep, send = stripe_part(flags, slots, pair, stats, gathered, other)
    for bit in bits[::-1]:
        total = keep + swapped(send, count, bit).astype(F32)
        half = total.shape[0] // 2
        keep, send = total[:half], total[half:].astype(BF16)
        if bit == 1:
            keep, send, coefs = lax.optimization_barrier((keep, send, coefs))
            grad_query, grad_key, grad_value, grad_mate, grad_across = gradient_part(
                flags, pair, own, mate_k, across_k, near_s, near_d, coefs, far_query
            )
        if bit == x_bit:
            keep, send, grad_across, grad_mate = lax.optimization_barrier(
                (keep, send, grad_across, grad_mate)
            )
            from_mate = swapped(grad_mate, count, 1)
            from_across = crossed(grad_across, count)
        if bit == bits[1]:
            keep, send, from_across = lax.optimization_barrier((keep, send, from_across))
    outs = []
    for which, grad_own in enumerate((grad_key, grad_value)):
        tail = jnp.pad(total[0, which], ((ROWS - STRIPE, 0), (0, 0)))
        outs.append(
            grad_own + from_mate[which].astype(F32) + from_across[which].astype(F32) + tail
        )
    return grad_query, outs[0], outs[1]


def solution(mesh):
    spec = P(("parts", "ctx"), None)
    return jax.shard_map(
        body,
        mesh=mesh,
        in_specs=(spec,) * 5,
        out_specs=(spec,) * 3,
        check_vma=False,
    )
```

```python
import jax
import jax.numpy as jnp
from jax import lax
from jax.experimental import pallas as pl
from jax.experimental.pallas import tpu as pltpu
from jax.sharding import PartitionSpec as P

HEAD_DIM = 64
BLOCK = 128
WIN = 2
STRIPE = 16
NCOL = 16
LANES = 128
ROWS = WIN * BLOCK
EXT = 3 * ROWS
FAR = NCOL * STRIPE
SPAN = (2 * WIN + 1) * BLOCK
SCALE = HEAD_DIM**-0.5
NT = (((1,), (1,)), ((), ()))
BF16, F32 = jnp.bfloat16, jnp.float32
SETS = 2


def tile(h, i):
    return slice((2 * h + i) * BLOCK, (2 * h + i + 1) * BLOCK)


def block_rows(i, flip):
    return pl.ds(pl.multiple_of((i ^ flip) * BLOCK, BLOCK), BLOCK)


def split_heads(ref, which, flip, two):
    first = lax.broadcasted_iota(jnp.int32, (BLOCK, LANES), 1) < HEAD_DIM
    for i in range(2):
        x = ref[which, block_rows(i, flip)]
        zero = jnp.zeros_like(x)
        two[tile(0, i)] = jnp.where(first, x, zero)
        two[tile(1, i)] = jnp.where(first, zero, x)


def both(i):
    return slice(2 * i * BLOCK, 2 * (i + 1) * BLOCK)


def stat(h, i):
    return tile(i, h)


def split_blocks(ref, which, flip, two):
    first = lax.broadcasted_iota(jnp.int32, (BLOCK, LANES), 1) < HEAD_DIM
    for i in range(2):
        x = ref[which, block_rows(i, flip)]
        zero = jnp.zeros_like(x)
        two[stat(0, i)] = jnp.where(first, x, zero)
        two[stat(1, i)] = jnp.where(first, zero, x)


def fill_window(flip, mate, own, which, across, ext):
    for i in range(2):
        rows = block_rows(i, flip)
        ext[tile(0, i)] = mate[rows]
        ext[tile(1, i)] = own[which, rows]
        ext[tile(2, i)] = across[rows]


def column_max(x):
    return jnp.max(x, axis=0, keepdims=True)


def column_sum(x):
    return jnp.sum(x, axis=0, keepdims=True)


def near_rows(i):
    return slice(i * BLOCK, i * BLOCK + SPAN)


def window_kernel(
    flags, biases, pair, own, mate_k, across_k, mate_v, across_v,
    near_s, near_d, stats,
    ext_k, ext_v, q_two, g_two,
):
    flip = flags[0]
    fill_window(flip, mate_k, own, 0, across_k, ext_k)
    fill_window(flip, mate_v, own, 1, across_v, ext_v)
    split_heads(pair, 0, flip, q_two)
    split_heads(pair, 1, flip, g_two)
    for h in range(2):
        heads = slice(h * ROWS, (h + 1) * ROWS)
        s = lax.dot_general(ext_k[...], q_two[heads], NT, preferred_element_type=F32)
        near_s[0, : 2 * ROWS, heads] = s[: 2 * ROWS]
        near_s[0, 2 * ROWS :, heads] = s[2 * ROWS :] + biases[0]
        near_d[0, :, heads] = lax.dot_general(
            ext_v[...], g_two[heads], NT, preferred_element_type=F32
        )
    for h in range(2):
        for i in range(2):
            s = near_s[0, near_rows(i), tile(h, i)]
            d = near_d[0, near_rows(i), tile(h, i)]
            top = column_max(s)
            u = jnp.exp(s - top)
            stats[0, 0:1, stat(h, i)] = top
            stats[0, 1:2, stat(h, i)] = column_sum(u)
            stats[0, 2:3, stat(h, i)] = column_sum(u * d)


def stripe_kernel(
    flags, slots, pair, stats, table_a, table_b, table_c, table_d,
    coefs, far_query, keep_a, keep_b, send_a, send_b,
    far_k, far_v, q_two, g_two, far_probs, far_scores, table_sum,
):
    flip = flags[0]
    part = table_a.shape[0]
    for i in range(2):
        for j in range(NCOL):
            slot = slots[i ^ flip, j]
            place = slot & (part - 1)
            rows = slice(j * STRIPE, (j + 1) * STRIPE)
            for which, far in ((0, far_k), (1, far_v)):
                far[i, rows] = jnp.where(
                    slot < 2 * part,
                    jnp.where(slot < part, table_a[place, which], table_b[place, which]),
                    jnp.where(slot < 3 * part, table_c[place, which], table_d[place, which]),
                )
    split_blocks(pair, 0, flip, q_two)
    split_blocks(pair, 1, flip, g_two)
    s, d = (
        jnp.concatenate(
            [
                lax.dot_general(far[i], two[both(i)], NT, preferred_element_type=F32)
                for i in range(2)
            ],
            axis=1,
        )
        for far, two in ((far_k, q_two), (far_v, g_two))
    )
    near_top = stats[0, 0:1]
    top = jnp.maximum(near_top, column_max(s))
    shrink = jnp.exp(near_top - top)
    u = jnp.exp(s - top)
    total = stats[0, 1:2] * shrink + column_sum(u)
    inv = 1.0 / total
    dot = (stats[0, 2:3] * shrink + column_sum(u * d)) * inv
    coefs[0, 0:1] = top + jnp.log(total)
    coefs[0, 1:2] = dot
    p = u * inv
    far_probs[...] = p.astype(BF16)
    far_scores[...] = (p * (d - dot)).astype(BF16)
    table_sum[...] = jnp.zeros_like(table_sum)
    for which, left, right in ((0, far_scores, q_two), (1, far_probs, g_two)):
        for i in range(2):
            far = jnp.dot(left[:, both(i)], right[both(i)], preferred_element_type=F32)
            parts = [far[j * STRIPE : (j + 1) * STRIPE] for j in range(NCOL)]
            places = [slots[i ^ flip, j] for j in range(NCOL)]
            if i == 1:
                parts = [x + table_sum[place, which] for x, place in zip(parts, places)]
            for x, place in zip(parts, places):
                table_sum[place, which] = x
    keep_a[...] = table_sum[:part]
    keep_b[...] = table_sum[part : 2 * part]
    send_a[...] = table_sum[2 * part : 3 * part].astype(send_a.dtype)
    send_b[...] = table_sum[3 * part :].astype(send_b.dtype)
    for i in range(2):
        out = jnp.dot(
            jnp.transpose(far_k[i]), far_scores[:, both(i)], preferred_element_type=F32
        )
        rows = slice(i * BLOCK, (i + 1) * BLOCK)
        far_query[0, :HEAD_DIM, rows] = out[:HEAD_DIM, :BLOCK]
        far_query[0, HEAD_DIM:, rows] = out[HEAD_DIM:, BLOCK:]


def gradient_kernel(
    flags, pair, own, mate_k, across_k, near_s, near_d, coefs, far_query,
    grad_query, grad_key, grad_value, grad_mate, grad_across,
    ext_k, q_two, g_two, probs, scores,
):
    flip = flags[0]
    fill_window(flip, mate_k, own, 0, across_k, ext_k)
    split_heads(pair, 0, flip, q_two)
    split_heads(pair, 1, flip, g_two)

    for h in range(2):
        for i in range(2):
            idle = slice((1 - i) * SPAN, (1 - i) * SPAN + BLOCK)
            probs[idle, tile(h, i)] = jnp.zeros((BLOCK, BLOCK), BF16)
            scores[idle, tile(h, i)] = jnp.zeros((BLOCK, BLOCK), BF16)

    for h in range(2):
        for i in range(2):
            rows = near_rows(i)
            p = jnp.exp(near_s[0, rows, tile(h, i)] - coefs[0, 0:1, stat(h, i)])
            probs[rows, tile(h, i)] = p.astype(BF16)
            ds = p * (near_d[0, rows, tile(h, i)] - coefs[0, 1:2, stat(h, i)])
            scores[rows, tile(h, i)] = ds.astype(BF16)
    for which, left, right, grad_own in (
        (0, scores, q_two, grad_key),
        (1, probs, g_two, grad_value),
    ):
        total = jnp.dot(left[...], right[...], preferred_element_type=F32)
        for i in range(2):
            rows = block_rows(i, flip)
            grad_mate[which, rows] = total[tile(0, i)].astype(grad_mate.dtype)
            grad_own[rows] = total[tile(1, i)]
            grad_across[which, rows] = total[tile(2, i)].astype(grad_across.dtype)
    k_t = jnp.transpose(ext_k[...])
    near = [
        jnp.dot(
            k_t[h * HEAD_DIM : (h + 1) * HEAD_DIM],
            scores[:, h * ROWS : (h + 1) * ROWS],
            preferred_element_type=F32,
        )
        for h in range(2)
    ]
    out = jnp.transpose(jnp.concatenate(near, axis=0) + far_query[0]) * SCALE
    for i in range(2):
        grad_query[block_rows(i, flip)] = out[i * BLOCK : (i + 1) * BLOCK]


SMEM_SPEC = pl.BlockSpec(memory_space=pltpu.SMEM)
VMEM_SPEC = pl.BlockSpec(memory_space=pltpu.VMEM)
TWO = pltpu.VMEM((2 * ROWS, LANES), BF16)
EXTENT = pltpu.VMEM((EXT, LANES), BF16)
FULL, ROW, PAIR, TABLE, STEP = "full", "row", "pair", "table", "step"


def view(ref, kind, p):
    lanes = pl.ds(p * LANES, LANES)
    if kind == ROW:
        return ref.at[:, lanes]
    if kind == PAIR:
        return ref.at[:, :, lanes]
    if kind == TABLE:
        return ref.at[:, :, :, lanes]
    if kind == STEP:
        return ref.at[pl.ds(p, 1)]
    return ref


def call(kernel, steps, in_kinds, out_kinds, out_shape, scratch, flops, moved, args):
    kinds = in_kinds + out_kinds

    def whole(*refs):
        for p in range(steps):
            views = [view(ref, kind, p) for ref, kind in zip(refs, kinds)]
            first = len(kinds) + p % SETS * len(scratch)
            kernel(*views, *refs[first : first + len(scratch)])

    return pl.pallas_call(
        whole,
        in_specs=[SMEM_SPEC if kind == FULL else VMEM_SPEC for kind in in_kinds],
        out_specs=[VMEM_SPEC] * len(out_kinds),
        out_shape=[jax.ShapeDtypeStruct(shape, dtype) for shape, dtype in out_shape],
        scratch_shapes=scratch * SETS,
        compiler_params=pltpu.CompilerParams(vmem_limit_bytes=24 << 20),
        cost_estimate=pl.CostEstimate(flops=flops, bytes_accessed=moved, transcendentals=1 << 20),
    )(*args)


def window_part(flags, biases, pair, own, mate_k, across_k, mate_v, across_v):
    steps = pair.shape[2] // LANES
    near = ((steps, EXT, 2 * ROWS), F32)
    return call(
        window_kernel,
        steps,
        [FULL, FULL, PAIR, PAIR, ROW, ROW, ROW, ROW],
        [STEP, STEP, STEP],
        [near, near, ((steps, 8, 2 * ROWS), F32)],
        [EXTENT, EXTENT, TWO, TWO],
        1 << 34,
        12 << 20,
        (flags, biases, pair, own, mate_k, across_k, mate_v, across_v),
    )


def stripe_part(flags, slots, pair, stats, *tables):
    part = tables[0].shape[0]
    width = pair.shape[2]
    steps = width // LANES
    return call(
        stripe_kernel,
        steps,
        [FULL, FULL, PAIR, STEP] + [TABLE] * 4,
        [STEP, STEP] + [TABLE] * 4,
        [((steps, 8, 2 * ROWS), F32), ((steps, LANES, ROWS), F32)]
        + [((part, 2, STRIPE, width), F32)] * 2
        + [((part, 2, STRIPE, width), BF16)] * 2,
        [
            pltpu.VMEM((2, FAR, LANES), BF16),
            pltpu.VMEM((2, FAR, LANES), BF16),
            TWO,
            TWO,
            pltpu.VMEM((FAR, 4 * BLOCK), BF16),
            pltpu.VMEM((FAR, 4 * BLOCK), BF16),
            pltpu.VMEM((4 * part, 2, STRIPE, LANES), F32),
        ],
        1 << 30,
        4 << 20,
        (flags, slots, pair, stats, *tables),
    )


def gradient_part(flags, pair, own, mate_k, across_k, near_s, near_d, coefs, far_query):
    width = pair.shape[2]
    steps = width // LANES
    return call(
        gradient_kernel,
        steps,
        [FULL, PAIR, PAIR, ROW, ROW, STEP, STEP, STEP, STEP],
        [ROW, ROW, ROW, PAIR, PAIR],
        [((ROWS, width), F32)] * 3 + [((2, ROWS, width), BF16)] * 2,
        [
            EXTENT,
            TWO,
            TWO,
            pltpu.VMEM((EXT, 2 * ROWS), BF16),
            pltpu.VMEM((EXT, 2 * ROWS), BF16),
        ],
        1 << 34,
        14 << 20,
        (flags, pair, own, mate_k, across_k, near_s, near_d, coefs, far_query),
    )


def stage_bits(count):
    bits = [1 << k for k in range(count.bit_length() - 1)]
    return bits[3:] + bits[2::-1]


def swapped(x, count, bit):
    return lax.ppermute(x, "ctx", [(i, i ^ bit) for i in range(count)])


def crossed(x, count):
    up = [(i, i + 1) for i in range(1, count - 1, 2)]
    return lax.ppermute(x, "ctx", up + [(j, i) for i, j in up])


def body(query_rows, key_rows, value_rows, grad_out, stripe_lists):
    count = lax.axis_size("ctx")
    me = lax.axis_index("ctx")
    bits = stage_bits(count)
    *z_bits, y_bit, x_bit, core_bit = bits
    relative = stripe_lists ^ me
    slots = jnp.zeros_like(relative)
    for place, bit in enumerate(bits):
        slots = slots | jnp.where((relative & bit) != 0, 1 << place, 0)
    flags = (1 - (me & 1)).reshape(1)
    alone = (me == 0) | (me == count - 1)
    biases = jnp.where(alone, -jnp.inf, 0.0).astype(F32).reshape(1)

    pair = jnp.stack([query_rows * BF16(SCALE), grad_out])
    own = jnp.stack([key_rows, value_rows])
    mate_k = swapped(key_rows, count, core_bit)
    mate_v = swapped(value_rows, count, core_bit)
    gathered = own[None, :, ROWS - STRIPE :]
    across_k = crossed(key_rows, count)
    for stage, bit in enumerate((*z_bits, y_bit)):
        if bit == y_bit:
            gathered, across_k = lax.optimization_barrier((gathered, across_k))
        gathered = jnp.concatenate([gathered, swapped(gathered, count, bit)], axis=0)
        if stage == 0:
            gathered, late = lax.optimization_barrier((gathered, value_rows))
            across_v = crossed(late, count)
    gathered, across_v = lax.optimization_barrier((gathered, across_v))
    near_s, near_d, stats = window_part(
        flags, biases, pair, own, mate_k, across_k, mate_v, across_v
    )
    beside = swapped(gathered, count, x_bit)
    beside, stats = lax.optimization_barrier((beside, stats))
    tables = [gathered, beside] + [swapped(x, count, core_bit) for x in (gathered, beside)]
    coefs, far_query, keep_a, keep_b, send_a, send_b = stripe_part(
        flags, slots, pair, stats, *tables
    )
    send = keep_b + swapped(send_b, count, core_bit).astype(F32)
    keep = keep_a + swapped(send_a, count, core_bit).astype(F32)
    send, coefs = lax.optimization_barrier((send.astype(BF16), coefs))
    grad_query, grad_key, grad_value, grad_mate, grad_across = gradient_part(
        flags, pair, own, mate_k, across_k, near_s, near_d, coefs, far_query
    )
    total = keep + swapped(send, count, x_bit).astype(F32)
    total, grad_mate = lax.optimization_barrier((total, grad_mate))
    from_mate = swapped(grad_mate, count, core_bit)
    from_across = crossed(grad_across, count)
    for bit in (y_bit, *z_bits[::-1]):
        half = total.shape[0] // 2
        keep, send = total[:half], total[half:].astype(BF16)
        if bit == z_bits[0]:
            keep, from_across = lax.optimization_barrier((keep, from_across))
        total = keep + swapped(send, count, bit).astype(F32)
    outs = []
    for which, grad_own in enumerate((grad_key, grad_value)):
        base = grad_own + from_mate[which].astype(F32) + from_across[which].astype(F32)
        base = lax.optimization_barrier(base)
        outs.append(base.at[ROWS - STRIPE :].add(total[0, which]))
    return grad_query, outs[0], outs[1]


def solution(mesh):
    spec = P(("parts", "ctx"), None)
    return jax.shard_map(
        body,
        mesh=mesh,
        in_specs=(spec,) * 5,
        out_specs=(spec,) * 3,
        check_vma=False,
    )
```

```python
import jax
import jax.numpy as jnp
from jax import lax
from jax.experimental import pallas as pl
from jax.experimental.pallas import tpu as pltpu
from jax.sharding import PartitionSpec as P

HEAD_DIM = 64
BLOCK = 128
WIN = 2
STRIPE = 16
NCOL = 16
LANES = 128
ROWS = WIN * BLOCK
EXT = 3 * ROWS
FAR = NCOL * STRIPE
SPAN = (2 * WIN + 1) * BLOCK
SCALE = HEAD_DIM**-0.5
NT = (((1,), (1,)), ((), ()))
BF16, F32 = jnp.bfloat16, jnp.float32


def tile(h, i):
    return slice((2 * h + i) * BLOCK, (2 * h + i + 1) * BLOCK)


def block_rows(i, flip):
    return pl.ds(pl.multiple_of((i ^ flip) * BLOCK, BLOCK), BLOCK)


def split_heads(ref, which, flip, two):
    first = lax.broadcasted_iota(jnp.int32, (BLOCK, LANES), 1) < HEAD_DIM
    for i in range(2):
        x = ref[which, block_rows(i, flip)]
        zero = jnp.zeros_like(x)
        two[tile(0, i)] = jnp.where(first, x, zero)
        two[tile(1, i)] = jnp.where(first, zero, x)


def both(i):
    return slice(2 * i * BLOCK, 2 * (i + 1) * BLOCK)


def stat(h, i):
    return tile(i, h)


def split_blocks(ref, which, flip, two):
    first = lax.broadcasted_iota(jnp.int32, (BLOCK, LANES), 1) < HEAD_DIM
    for i in range(2):
        x = ref[which, block_rows(i, flip)]
        zero = jnp.zeros_like(x)
        two[stat(0, i)] = jnp.where(first, x, zero)
        two[stat(1, i)] = jnp.where(first, zero, x)


def fill_window(flip, mate, own, which, across, ext):
    for i in range(2):
        rows = block_rows(i, flip)
        ext[tile(0, i)] = mate[rows]
        ext[tile(1, i)] = own[which, rows]
        ext[tile(2, i)] = across[rows]


def column_max(x):
    return jnp.max(x, axis=0, keepdims=True)


def column_sum(x):
    return jnp.sum(x, axis=0, keepdims=True)


def near_rows(i):
    return slice(i * BLOCK, i * BLOCK + SPAN)


def window_products(
    flags, biases, pair, own, mate_k, across_k, mate_v, across_v,
    near_s, near_d, stats,
    ext_k, ext_v, q_two, g_two,
):
    flip = flags[0]
    fill_window(flip, mate_k, own, 0, across_k, ext_k)
    fill_window(flip, mate_v, own, 1, across_v, ext_v)
    split_heads(pair, 0, flip, q_two)
    split_heads(pair, 1, flip, g_two)
    for h in range(2):
        heads = slice(h * ROWS, (h + 1) * ROWS)
        s = lax.dot_general(ext_k[...], q_two[heads], NT, preferred_element_type=F32)
        near_s[0, : 2 * ROWS, heads] = s[: 2 * ROWS]
        near_s[0, 2 * ROWS :, heads] = s[2 * ROWS :] + biases[0]
        near_d[0, :, heads] = lax.dot_general(
            ext_v[...], g_two[heads], NT, preferred_element_type=F32
        )


def window_stats(
    flags, biases, pair, own, mate_k, across_k, mate_v, across_v,
    near_s, near_d, stats,
    ext_k, ext_v, q_two, g_two,
):
    for h in range(2):
        for i in range(2):
            s = near_s[0, near_rows(i), tile(h, i)]
            d = near_d[0, near_rows(i), tile(h, i)]
            top = column_max(s)
            u = jnp.exp(s - top)
            stats[0, 0:1, stat(h, i)] = top
            stats[0, 1:2, stat(h, i)] = column_sum(u)
            stats[0, 2:3, stat(h, i)] = column_sum(u * d)


def stripe_products(
    flags, slots, pair, stats, table_a, table_b, table_c, table_d,
    coefs, far_query, keep_a, keep_b, send_a, send_b,
    far_k, far_v, q_two, g_two, far_s, far_d, far_probs, far_scores, table_sum,
):
    flip = flags[0]
    part = table_a.shape[0]
    for i in range(2):
        for j in range(NCOL):
            slot = slots[i ^ flip, j]
            place = slot & (part - 1)
            rows = slice(j * STRIPE, (j + 1) * STRIPE)
            for which, far in ((0, far_k), (1, far_v)):
                far[i, rows] = jnp.where(
                    slot < 2 * part,
                    jnp.where(slot < part, table_a[place, which], table_b[place, which]),
                    jnp.where(slot < 3 * part, table_c[place, which], table_d[place, which]),
                )
    split_blocks(pair, 0, flip, q_two)
    split_blocks(pair, 1, flip, g_two)
    for far, two, out in ((far_k, q_two, far_s), (far_v, g_two, far_d)):
        for i in range(2):
            out[:, both(i)] = lax.dot_general(
                far[i], two[both(i)], NT, preferred_element_type=F32
            )


def stripe_probs(
    flags, slots, pair, stats, table_a, table_b, table_c, table_d,
    coefs, far_query, keep_a, keep_b, send_a, send_b,
    far_k, far_v, q_two, g_two, far_s, far_d, far_probs, far_scores, table_sum,
):
    s, d = far_s[...], far_d[...]
    near_top = stats[0, 0:1]
    top = jnp.maximum(near_top, column_max(s))
    shrink = jnp.exp(near_top - top)
    u = jnp.exp(s - top)
    total = stats[0, 1:2] * shrink + column_sum(u)
    inv = 1.0 / total
    dot = (stats[0, 2:3] * shrink + column_sum(u * d)) * inv
    coefs[0, 0:1] = top + jnp.log(total)
    coefs[0, 1:2] = dot
    p = u * inv
    far_probs[...] = p.astype(BF16)
    far_scores[...] = (p * (d - dot)).astype(BF16)


def stripe_gradients(
    flags, slots, pair, stats, table_a, table_b, table_c, table_d,
    coefs, far_query, keep_a, keep_b, send_a, send_b,
    far_k, far_v, q_two, g_two, far_s, far_d, far_probs, far_scores, table_sum,
):
    flip = flags[0]
    part = table_a.shape[0]
    table_sum[...] = jnp.zeros_like(table_sum)
    for which, left, right in ((0, far_scores, q_two), (1, far_probs, g_two)):
        for i in range(2):
            far = jnp.dot(left[:, both(i)], right[both(i)], preferred_element_type=F32)
            parts = [far[j * STRIPE : (j + 1) * STRIPE] for j in range(NCOL)]
            places = [slots[i ^ flip, j] for j in range(NCOL)]
            if i == 1:
                parts = [x + table_sum[place, which] for x, place in zip(parts, places)]
            for x, place in zip(parts, places):
                table_sum[place, which] = x
    keep_a[...] = table_sum[:part]
    keep_b[...] = table_sum[part : 2 * part]
    send_a[...] = table_sum[2 * part : 3 * part].astype(send_a.dtype)
    send_b[...] = table_sum[3 * part :].astype(send_b.dtype)
    for i in range(2):
        out = jnp.dot(
            jnp.transpose(far_k[i]), far_scores[:, both(i)], preferred_element_type=F32
        )
        rows = slice(i * BLOCK, (i + 1) * BLOCK)
        far_query[0, :HEAD_DIM, rows] = out[:HEAD_DIM, :BLOCK]
        far_query[0, HEAD_DIM:, rows] = out[HEAD_DIM:, BLOCK:]


def window_probs(
    flags, pair, own, mate_k, across_k, near_s, near_d, coefs, far_query,
    grad_query, grad_key, grad_value, grad_mate, across_k_out, across_v_out,
    ext_k, q_two, g_two, probs, scores,
):
    flip = flags[0]
    fill_window(flip, mate_k, own, 0, across_k, ext_k)
    split_heads(pair, 0, flip, q_two)
    split_heads(pair, 1, flip, g_two)

    for h in range(2):
        for i in range(2):
            idle = slice((1 - i) * SPAN, (1 - i) * SPAN + BLOCK)
            probs[idle, tile(h, i)] = jnp.zeros((BLOCK, BLOCK), BF16)
            scores[idle, tile(h, i)] = jnp.zeros((BLOCK, BLOCK), BF16)

    for h in range(2):
        for i in range(2):
            rows = near_rows(i)
            p = jnp.exp(near_s[0, rows, tile(h, i)] - coefs[0, 0:1, stat(h, i)])
            probs[rows, tile(h, i)] = p.astype(BF16)
            ds = p * (near_d[0, rows, tile(h, i)] - coefs[0, 1:2, stat(h, i)])
            scores[rows, tile(h, i)] = ds.astype(BF16)


def window_gradients(
    flags, pair, own, mate_k, across_k, near_s, near_d, coefs, far_query,
    grad_query, grad_key, grad_value, grad_mate, across_k_out, across_v_out,
    ext_k, q_two, g_two, probs, scores,
):
    flip = flags[0]
    for which, left, right, grad_own, grad_across in (
        (1, probs, g_two, grad_value, across_v_out),
        (0, scores, q_two, grad_key, across_k_out),
    ):
        total = jnp.dot(left[...], right[...], preferred_element_type=F32)
        for i in range(2):
            rows = block_rows(i, flip)
            grad_mate[which, rows] = total[tile(0, i)].astype(grad_mate.dtype)
            grad_own[rows] = total[tile(1, i)]
            grad_across[rows] = total[tile(2, i)].astype(grad_across.dtype)
    k_t = jnp.transpose(ext_k[...])
    near = [
        jnp.dot(
            k_t[h * HEAD_DIM : (h + 1) * HEAD_DIM],
            scores[:, h * ROWS : (h + 1) * ROWS],
            preferred_element_type=F32,
        )
        for h in range(2)
    ]
    out = jnp.transpose(jnp.concatenate(near, axis=0) + far_query[0]) * SCALE
    for i in range(2):
        grad_query[block_rows(i, flip)] = out[i * BLOCK : (i + 1) * BLOCK]


SMEM_SPEC = pl.BlockSpec(memory_space=pltpu.SMEM)
VMEM_SPEC = pl.BlockSpec(memory_space=pltpu.VMEM)
TWO = pltpu.VMEM((2 * ROWS, LANES), BF16)
EXTENT = pltpu.VMEM((EXT, LANES), BF16)
FULL, ROW, PAIR, TABLE, STEP = "full", "row", "pair", "table", "step"


def view(ref, kind, p):
    lanes = pl.ds(p * LANES, LANES)
    if kind == ROW:
        return ref.at[:, lanes]
    if kind == PAIR:
        return ref.at[:, :, lanes]
    if kind == TABLE:
        return ref.at[:, :, :, lanes]
    if kind == STEP:
        return ref.at[pl.ds(p, 1)]
    return ref


def call(phases, steps, in_kinds, out_kinds, out_shape, scratch, flops, moved, args):
    kinds = in_kinds + out_kinds

    def whole(*refs):
        for phase in phases:
            for p in range(steps):
                views = [view(ref, kind, p) for ref, kind in zip(refs, kinds)]
                first = len(kinds) + p * len(scratch)
                phase(*views, *refs[first : first + len(scratch)])

    return pl.pallas_call(
        whole,
        in_specs=[SMEM_SPEC if kind == FULL else VMEM_SPEC for kind in in_kinds],
        out_specs=[VMEM_SPEC] * len(out_kinds),
        out_shape=[jax.ShapeDtypeStruct(shape, dtype) for shape, dtype in out_shape],
        scratch_shapes=scratch * steps,
        compiler_params=pltpu.CompilerParams(vmem_limit_bytes=32 << 20),
        cost_estimate=pl.CostEstimate(flops=flops, bytes_accessed=moved, transcendentals=1 << 20),
    )(*args)


def window_part(flags, biases, pair, own, mate_k, across_k, mate_v, across_v):
    steps = pair.shape[2] // LANES
    near = ((steps, EXT, 2 * ROWS), F32)
    return call(
        (window_products, window_stats),
        steps,
        [FULL, FULL, PAIR, PAIR, ROW, ROW, ROW, ROW],
        [STEP, STEP, STEP],
        [near, near, ((steps, 8, 2 * ROWS), F32)],
        [EXTENT, EXTENT, TWO, TWO],
        1 << 34,
        12 << 20,
        (flags, biases, pair, own, mate_k, across_k, mate_v, across_v),
    )


def stripe_part(flags, slots, pair, stats, *tables):
    part = tables[0].shape[0]
    width = pair.shape[2]
    steps = width // LANES
    return call(
        (stripe_products, stripe_probs, stripe_gradients),
        steps,
        [FULL, FULL, PAIR, STEP] + [TABLE] * 4,
        [STEP, STEP] + [TABLE] * 4,
        [((steps, 8, 2 * ROWS), F32), ((steps, LANES, ROWS), F32)]
        + [((part, 2, STRIPE, width), F32)] * 2
        + [((part, 2, STRIPE, width), BF16)] * 2,
        [
            pltpu.VMEM((2, FAR, LANES), BF16),
            pltpu.VMEM((2, FAR, LANES), BF16),
            TWO,
            TWO,
            pltpu.VMEM((FAR, 4 * BLOCK), F32),
            pltpu.VMEM((FAR, 4 * BLOCK), F32),
            pltpu.VMEM((FAR, 4 * BLOCK), BF16),
            pltpu.VMEM((FAR, 4 * BLOCK), BF16),
            pltpu.VMEM((4 * part, 2, STRIPE, LANES), F32),
        ],
        1 << 30,
        4 << 20,
        (flags, slots, pair, stats, *tables),
    )


def gradient_part(flags, pair, own, mate_k, across_k, near_s, near_d, coefs, far_query):
    width = pair.shape[2]
    steps = width // LANES
    return call(
        (window_probs, window_gradients),
        steps,
        [FULL, PAIR, PAIR, ROW, ROW, STEP, STEP, STEP, STEP],
        [ROW, ROW, ROW, PAIR, ROW, ROW],
        [((ROWS, width), F32)] * 3 + [((2, ROWS, width), BF16)] + [((ROWS, width), BF16)] * 2,
        [
            EXTENT,
            TWO,
            TWO,
            pltpu.VMEM((EXT, 2 * ROWS), BF16),
            pltpu.VMEM((EXT, 2 * ROWS), BF16),
        ],
        1 << 30,
        1 << 20,
        (flags, pair, own, mate_k, across_k, near_s, near_d, coefs, far_query),
    )


def stage_bits(count):
    bits = [1 << k for k in range(count.bit_length() - 1)]
    return bits[3:] + bits[2::-1]


def swapped(x, count, bit):
    return lax.ppermute(x, "ctx", [(i, i ^ bit) for i in range(count)])


def crossed(x, count):
    up = [(i, i + 1) for i in range(1, count - 1, 2)]
    return lax.ppermute(x, "ctx", up + [(j, i) for i, j in up])


def body(query_rows, key_rows, value_rows, grad_out, stripe_lists):
    count = lax.axis_size("ctx")
    me = lax.axis_index("ctx")
    bits = stage_bits(count)
    *z_bits, y_bit, x_bit, core_bit = bits
    relative = stripe_lists ^ me
    slots = jnp.zeros_like(relative)
    for place, bit in enumerate(bits):
        slots = slots | jnp.where((relative & bit) != 0, 1 << place, 0)
    flags = (1 - (me & 1)).reshape(1)
    alone = (me == 0) | (me == count - 1)
    biases = jnp.where(alone, -jnp.inf, 0.0).astype(F32).reshape(1)

    pair = jnp.stack([query_rows * BF16(SCALE), grad_out])
    own = jnp.stack([key_rows, value_rows])
    mate_k = swapped(key_rows, count, core_bit)
    mate_v = swapped(value_rows, count, core_bit)
    gathered = own[None, :, ROWS - STRIPE :]
    across_k = crossed(key_rows, count)
    for stage, bit in enumerate((*z_bits, y_bit)):
        if bit == y_bit:
            gathered, across_k = lax.optimization_barrier((gathered, across_k))
        gathered = jnp.concatenate([gathered, swapped(gathered, count, bit)], axis=0)
        if stage == 0:
            gathered, late = lax.optimization_barrier((gathered, value_rows))
            across_v = crossed(late, count)
    gathered, across_v = lax.optimization_barrier((gathered, across_v))
    near_s, near_d, stats = window_part(
        flags, biases, pair, own, mate_k, across_k, mate_v, across_v
    )
    beside = swapped(gathered, count, x_bit)
    beside, stats = lax.optimization_barrier((beside, stats))
    tables = [gathered, beside] + [swapped(x, count, core_bit) for x in (gathered, beside)]
    coefs, far_query, keep_a, keep_b, send_a, send_b = stripe_part(
        flags, slots, pair, stats, *tables
    )
    send = keep_b + swapped(send_b, count, core_bit).astype(F32)
    keep = keep_a + swapped(send_a, count, core_bit).astype(F32)
    send, coefs = lax.optimization_barrier((send.astype(BF16), coefs))
    grad_query, grad_key, grad_value, grad_mate, out_k, out_v = gradient_part(
        flags, pair, own, mate_k, across_k, near_s, near_d, coefs, far_query
    )
    from_v, from_k = crossed(out_v, count), crossed(out_k, count)
    total = keep + swapped(send, count, x_bit).astype(F32)
    total, grad_mate = lax.optimization_barrier((total, grad_mate))
    from_mate = swapped(grad_mate, count, core_bit)
    for bit in (y_bit, *z_bits[::-1]):
        half = total.shape[0] // 2
        keep, send = total[:half], total[half:].astype(BF16)
        if bit == z_bits[-1]:
            keep, from_v = lax.optimization_barrier((keep, from_v))
        if bit == z_bits[0]:
            keep, from_k = lax.optimization_barrier((keep, from_k))
        total = keep + swapped(send, count, bit).astype(F32)
    outs = []
    for which, grad_own in enumerate((grad_key, grad_value)):
        base = grad_own + from_mate[which].astype(F32) + (from_k, from_v)[which].astype(F32)
        base = lax.optimization_barrier(base)
        outs.append(base.at[ROWS - STRIPE :].add(total[0, which]))
    return grad_query, outs[0], outs[1]


def solution(mesh):
    spec = P(("parts", "ctx"), None)
    return jax.shard_map(
        body,
        mesh=mesh,
        in_specs=(spec,) * 5,
        out_specs=(spec,) * 3,
        check_vma=False,
    )
```

```python
import jax
import jax.numpy as jnp
from jax import lax
from jax.experimental import pallas as pl
from jax.experimental.pallas import tpu as pltpu
from jax.sharding import PartitionSpec as P

HEAD_DIM = 64
BLOCK = 128
WIN = 2
STRIPE = 16
NCOL = 16
LANES = 128
ROWS = WIN * BLOCK
EXT = 3 * ROWS
FAR = NCOL * STRIPE
SPAN = (2 * WIN + 1) * BLOCK
SCALE = HEAD_DIM**-0.5
NT = (((1,), (1,)), ((), ()))
BF16, F32 = jnp.bfloat16, jnp.float32


def tile(h, i):
    return slice((2 * h + i) * BLOCK, (2 * h + i + 1) * BLOCK)


def block_rows(i, flip):
    return pl.ds(pl.multiple_of((i ^ flip) * BLOCK, BLOCK), BLOCK)


def split_heads(ref, which, flip, two):
    first = lax.broadcasted_iota(jnp.int32, (BLOCK, LANES), 1) < HEAD_DIM
    for i in range(2):
        x = ref[which, block_rows(i, flip)]
        zero = jnp.zeros_like(x)
        two[tile(0, i)] = jnp.where(first, x, zero)
        two[tile(1, i)] = jnp.where(first, zero, x)


def both(i):
    return slice(2 * i * BLOCK, 2 * (i + 1) * BLOCK)


def stat(h, i):
    return tile(i, h)


def split_blocks(ref, which, flip, two):
    first = lax.broadcasted_iota(jnp.int32, (BLOCK, LANES), 1) < HEAD_DIM
    for i in range(2):
        x = ref[which, block_rows(i, flip)]
        zero = jnp.zeros_like(x)
        two[stat(0, i)] = jnp.where(first, x, zero)
        two[stat(1, i)] = jnp.where(first, zero, x)


def fill_window(flip, mate, own, which, across, ext):
    for i in range(2):
        rows = block_rows(i, flip)
        ext[tile(0, i)] = mate[rows]
        ext[tile(1, i)] = own[which, rows]
        ext[tile(2, i)] = across[rows]


def column_max(x):
    return jnp.max(x, axis=0, keepdims=True)


def column_sum(x):
    return jnp.sum(x, axis=0, keepdims=True)


def near_rows(i):
    return slice(i * BLOCK, i * BLOCK + SPAN)


def window_products(
    flags, biases, pair, own, mate_k, across_k, mate_v, across_v,
    near_s, near_d, stats,
    ext_k, ext_v, q_two, g_two,
):
    flip = flags[0]
    fill_window(flip, mate_k, own, 0, across_k, ext_k)
    fill_window(flip, mate_v, own, 1, across_v, ext_v)
    split_heads(pair, 0, flip, q_two)
    split_heads(pair, 1, flip, g_two)
    for h in range(2):
        heads = slice(h * ROWS, (h + 1) * ROWS)
        s = lax.dot_general(ext_k[...], q_two[heads], NT, preferred_element_type=F32)
        near_s[0, : 2 * ROWS, heads] = s[: 2 * ROWS]
        near_s[0, 2 * ROWS :, heads] = s[2 * ROWS :] + biases[0]
        near_d[0, :, heads] = lax.dot_general(
            ext_v[...], g_two[heads], NT, preferred_element_type=F32
        )


def window_stats(
    flags, biases, pair, own, mate_k, across_k, mate_v, across_v,
    near_s, near_d, stats,
    ext_k, ext_v, q_two, g_two,
):
    for h in range(2):
        for i in range(2):
            s = near_s[0, near_rows(i), tile(h, i)]
            d = near_d[0, near_rows(i), tile(h, i)]
            top = column_max(s)
            u = jnp.exp(s - top)
            stats[0, 0:1, stat(h, i)] = top
            stats[0, 1:2, stat(h, i)] = column_sum(u)
            stats[0, 2:3, stat(h, i)] = column_sum(u * d)


def stripe_products(
    flags, slots, pair, stats, table_a, table_b, table_c, table_d,
    coefs, far_query, keep_a, keep_b, send_a, send_b,
    far_k, far_v, q_two, g_two, far_s, far_d, far_probs, far_scores, table_sum,
):
    flip = flags[0]
    part = table_a.shape[0]
    for i in range(2):
        for j in range(NCOL):
            slot = slots[0, i ^ flip, j]
            place = slot & (part - 1)
            rows = slice(j * STRIPE, (j + 1) * STRIPE)
            for which, far in ((0, far_k), (1, far_v)):
                far[i, rows] = jnp.where(
                    slot < 2 * part,
                    jnp.where(slot < part, table_a[place, which], table_b[place, which]),
                    jnp.where(slot < 3 * part, table_c[place, which], table_d[place, which]),
                )
    split_blocks(pair, 0, flip, q_two)
    split_blocks(pair, 1, flip, g_two)
    for far, two, out in ((far_k, q_two, far_s), (far_v, g_two, far_d)):
        for i in range(2):
            out[:, both(i)] = lax.dot_general(
                far[i], two[both(i)], NT, preferred_element_type=F32
            )


def stripe_probs(
    flags, slots, pair, stats, table_a, table_b, table_c, table_d,
    coefs, far_query, keep_a, keep_b, send_a, send_b,
    far_k, far_v, q_two, g_two, far_s, far_d, far_probs, far_scores, table_sum,
):
    s, d = far_s[...], far_d[...]
    near_top = stats[0, 0:1]
    top = jnp.maximum(near_top, column_max(s))
    shrink = jnp.exp(near_top - top)
    u = jnp.exp(s - top)
    total = stats[0, 1:2] * shrink + column_sum(u)
    inv = 1.0 / total
    dot = (stats[0, 2:3] * shrink + column_sum(u * d)) * inv
    coefs[0, 0:1] = top + jnp.log(total)
    coefs[0, 1:2] = dot
    p = u * inv
    far_probs[...] = p.astype(BF16)
    far_scores[...] = (p * (d - dot)).astype(BF16)


def stripe_gradients(
    flags, slots, pair, stats, table_a, table_b, table_c, table_d,
    coefs, far_query, keep_a, keep_b, send_a, send_b,
    far_k, far_v, q_two, g_two, far_s, far_d, far_probs, far_scores, table_sum,
):
    flip = flags[0]
    part = table_a.shape[0]
    table_sum[...] = jnp.zeros_like(table_sum)
    for which, left, right in ((0, far_scores, q_two), (1, far_probs, g_two)):
        for i in range(2):
            far = jnp.dot(left[:, both(i)], right[both(i)], preferred_element_type=F32)
            parts = [far[j * STRIPE : (j + 1) * STRIPE] for j in range(NCOL)]
            places = [slots[1, i ^ flip, j] for j in range(NCOL)]
            if i == 1:
                parts = [x + table_sum[place, which] for x, place in zip(parts, places)]
            for x, place in zip(parts, places):
                table_sum[place, which] = x
    keep_a[...] = table_sum[:part]
    keep_b[...] = table_sum[part : 2 * part]
    send_a[...] = table_sum[2 * part : 3 * part].astype(send_a.dtype)
    send_b[...] = table_sum[3 * part :].astype(send_b.dtype)
    for i in range(2):
        out = jnp.dot(
            jnp.transpose(far_k[i]), far_scores[:, both(i)], preferred_element_type=F32
        )
        rows = slice(i * BLOCK, (i + 1) * BLOCK)
        far_query[0, :HEAD_DIM, rows] = out[:HEAD_DIM, :BLOCK]
        far_query[0, HEAD_DIM:, rows] = out[HEAD_DIM:, BLOCK:]


def window_probs(
    flags, pair, own, mate_k, across_k, near_s, near_d, coefs, far_query,
    grad_query, grad_key, grad_value, grad_mate, across_k_out, across_v_out,
    ext_k, q_two, g_two, probs, scores,
):
    flip = flags[0]
    fill_window(flip, mate_k, own, 0, across_k, ext_k)
    split_heads(pair, 0, flip, q_two)
    split_heads(pair, 1, flip, g_two)

    for h in range(2):
        for i in range(2):
            idle = slice((1 - i) * SPAN, (1 - i) * SPAN + BLOCK)
            probs[idle, tile(h, i)] = jnp.zeros((BLOCK, BLOCK), BF16)
            scores[idle, tile(h, i)] = jnp.zeros((BLOCK, BLOCK), BF16)

    for h in range(2):
        for i in range(2):
            rows = near_rows(i)
            p = jnp.exp(near_s[0, rows, tile(h, i)] - coefs[0, 0:1, stat(h, i)])
            probs[rows, tile(h, i)] = p.astype(BF16)
            ds = p * (near_d[0, rows, tile(h, i)] - coefs[0, 1:2, stat(h, i)])
            scores[rows, tile(h, i)] = ds.astype(BF16)


def window_gradients(
    flags, pair, own, mate_k, across_k, near_s, near_d, coefs, far_query,
    grad_query, grad_key, grad_value, grad_mate, across_k_out, across_v_out,
    ext_k, q_two, g_two, probs, scores,
):
    flip = flags[0]
    for which, left, right, grad_own, grad_across in (
        (1, probs, g_two, grad_value, across_v_out),
        (0, scores, q_two, grad_key, across_k_out),
    ):
        total = jnp.dot(left[...], right[...], preferred_element_type=F32)
        for i in range(2):
            rows = block_rows(i, flip)
            grad_mate[which, rows] = total[tile(0, i)].astype(grad_mate.dtype)
            grad_own[rows] = total[tile(1, i)]
            grad_across[rows] = total[tile(2, i)].astype(grad_across.dtype)
    k_t = jnp.transpose(ext_k[...])
    near = [
        jnp.dot(
            k_t[h * HEAD_DIM : (h + 1) * HEAD_DIM],
            scores[:, h * ROWS : (h + 1) * ROWS],
            preferred_element_type=F32,
        )
        for h in range(2)
    ]
    out = jnp.transpose(jnp.concatenate(near, axis=0) + far_query[0]) * SCALE
    for i in range(2):
        grad_query[block_rows(i, flip)] = out[i * BLOCK : (i + 1) * BLOCK]


SMEM_SPEC = pl.BlockSpec(memory_space=pltpu.SMEM)
VMEM_SPEC = pl.BlockSpec(memory_space=pltpu.VMEM)
TWO = pltpu.VMEM((2 * ROWS, LANES), BF16)
EXTENT = pltpu.VMEM((EXT, LANES), BF16)
FULL, ROW, PAIR, TABLE, STEP = "full", "row", "pair", "table", "step"


def view(ref, kind, p):
    lanes = pl.ds(p * LANES, LANES)
    if kind == ROW:
        return ref.at[:, lanes]
    if kind == PAIR:
        return ref.at[:, :, lanes]
    if kind == TABLE:
        return ref.at[:, :, :, lanes]
    if kind == STEP:
        return ref.at[pl.ds(p, 1)]
    return ref


def call(phases, steps, in_kinds, out_kinds, out_shape, scratch, flops, moved, args):
    kinds = in_kinds + out_kinds

    def whole(*refs):
        for phase in phases:
            for p in range(steps):
                views = [view(ref, kind, p) for ref, kind in zip(refs, kinds)]
                first = len(kinds) + p * len(scratch)
                phase(*views, *refs[first : first + len(scratch)])

    return pl.pallas_call(
        whole,
        in_specs=[SMEM_SPEC if kind == FULL else VMEM_SPEC for kind in in_kinds],
        out_specs=[VMEM_SPEC] * len(out_kinds),
        out_shape=[jax.ShapeDtypeStruct(shape, dtype) for shape, dtype in out_shape],
        scratch_shapes=scratch * steps,
        compiler_params=pltpu.CompilerParams(vmem_limit_bytes=32 << 20),
        cost_estimate=pl.CostEstimate(flops=flops, bytes_accessed=moved, transcendentals=1 << 20),
    )(*args)


def window_part(flags, biases, pair, own, mate_k, across_k, mate_v, across_v):
    steps = pair.shape[2] // LANES
    near = ((steps, EXT, 2 * ROWS), F32)
    return call(
        (window_products, window_stats),
        steps,
        [FULL, FULL, PAIR, PAIR, ROW, ROW, ROW, ROW],
        [STEP, STEP, STEP],
        [near, near, ((steps, 8, 2 * ROWS), F32)],
        [EXTENT, EXTENT, TWO, TWO],
        1 << 34,
        12 << 20,
        (flags, biases, pair, own, mate_k, across_k, mate_v, across_v),
    )


def stripe_part(flags, slots, pair, stats, *tables):
    part = tables[0].shape[0]
    width = pair.shape[2]
    steps = width // LANES
    return call(
        (stripe_products, stripe_probs, stripe_gradients),
        steps,
        [FULL, FULL, PAIR, STEP] + [TABLE] * 4,
        [STEP, STEP] + [TABLE] * 4,
        [((steps, 8, 2 * ROWS), F32), ((steps, LANES, ROWS), F32)]
        + [((part, 2, STRIPE, width), F32)] * 2
        + [((part, 2, STRIPE, width), BF16)] * 2,
        [
            pltpu.VMEM((2, FAR, LANES), BF16),
            pltpu.VMEM((2, FAR, LANES), BF16),
            TWO,
            TWO,
            pltpu.VMEM((FAR, 4 * BLOCK), F32),
            pltpu.VMEM((FAR, 4 * BLOCK), F32),
            pltpu.VMEM((FAR, 4 * BLOCK), BF16),
            pltpu.VMEM((FAR, 4 * BLOCK), BF16),
            pltpu.VMEM((4 * part, 2, STRIPE, LANES), F32),
        ],
        1 << 30,
        4 << 20,
        (flags, slots, pair, stats, *tables),
    )


def gradient_part(flags, pair, own, mate_k, across_k, near_s, near_d, coefs, far_query):
    width = pair.shape[2]
    steps = width // LANES
    return call(
        (window_probs, window_gradients),
        steps,
        [FULL, PAIR, PAIR, ROW, ROW, STEP, STEP, STEP, STEP],
        [ROW, ROW, ROW, PAIR, ROW, ROW],
        [((ROWS, width), F32)] * 3 + [((2, ROWS, width), BF16)] + [((ROWS, width), BF16)] * 2,
        [
            EXTENT,
            TWO,
            TWO,
            pltpu.VMEM((EXT, 2 * ROWS), BF16),
            pltpu.VMEM((EXT, 2 * ROWS), BF16),
        ],
        1 << 30,
        1 << 20,
        (flags, pair, own, mate_k, across_k, near_s, near_d, coefs, far_query),
    )


def stage_bits(count):
    bits = [1 << k for k in range(count.bit_length() - 1)]
    return bits[3:] + bits[2::-1]


def swapped(x, count, bit):
    return lax.ppermute(x, "ctx", [(i, i ^ bit) for i in range(count)])


def crossed(x, count):
    up = [(i, i + 1) for i in range(1, count - 1, 2)]
    return lax.ppermute(x, "ctx", up + [(j, i) for i, j in up])


def body(query_rows, key_rows, value_rows, grad_out, stripe_lists):
    count = lax.axis_size("ctx")
    me = lax.axis_index("ctx")
    bits = stage_bits(count)
    *z_bits, y_bit, x_bit, core_bit = bits
    relative = stripe_lists ^ me
    slots = jnp.stack(
        [
            sum(jnp.where((relative & bit) != 0, 1 << place, 0) for place, bit in enumerate(order))
            for order in ((*z_bits, y_bit, x_bit, core_bit), (*z_bits, x_bit, y_bit, core_bit))
        ]
    )
    flags = (1 - (me & 1)).reshape(1)
    alone = (me == 0) | (me == count - 1)
    biases = jnp.where(alone, -jnp.inf, 0.0).astype(F32).reshape(1)

    pair = jnp.stack([query_rows * BF16(SCALE), grad_out])
    own = jnp.stack([key_rows, value_rows])
    mate_k = swapped(key_rows, count, core_bit)
    mate_v = swapped(value_rows, count, core_bit)
    gathered = own[None, :, ROWS - STRIPE :]
    across_k = crossed(key_rows, count)
    for stage, bit in enumerate((*z_bits, y_bit)):
        if bit == y_bit:
            gathered, across_k = lax.optimization_barrier((gathered, across_k))
        gathered = jnp.concatenate([gathered, swapped(gathered, count, bit)], axis=0)
        if stage == 0:
            gathered, late = lax.optimization_barrier((gathered, value_rows))
            across_v = crossed(late, count)
    gathered, across_v = lax.optimization_barrier((gathered, across_v))
    near_s, near_d, stats = window_part(
        flags, biases, pair, own, mate_k, across_k, mate_v, across_v
    )
    beside = swapped(gathered, count, x_bit)
    beside, stats = lax.optimization_barrier((beside, stats))
    tables = [gathered, beside] + [swapped(x, count, core_bit) for x in (gathered, beside)]
    coefs, far_query, keep_a, keep_b, send_a, send_b = stripe_part(
        flags, slots, pair, stats, *tables
    )
    send = keep_b + swapped(send_b, count, core_bit).astype(F32)
    keep = keep_a + swapped(send_a, count, core_bit).astype(F32)
    send, coefs = lax.optimization_barrier((send.astype(BF16), coefs))
    grad_query, grad_key, grad_value, grad_mate, out_k, out_v = gradient_part(
        flags, pair, own, mate_k, across_k, near_s, near_d, coefs, far_query
    )
    from_v, from_k = crossed(out_v, count), crossed(out_k, count)
    total = keep + swapped(send, count, y_bit).astype(F32)
    total, grad_mate = lax.optimization_barrier((total, grad_mate))
    from_mate = swapped(grad_mate, count, core_bit)
    for bit in (x_bit, *z_bits[::-1]):
        half = total.shape[0] // 2
        keep, send = total[:half], total[half:].astype(BF16)
        if bit == z_bits[-1]:
            keep, from_v = lax.optimization_barrier((keep, from_v))
        if bit == z_bits[0]:
            keep, from_k = lax.optimization_barrier((keep, from_k))
        total = keep + swapped(send, count, bit).astype(F32)
    outs = []
    for which, grad_own in enumerate((grad_key, grad_value)):
        base = grad_own + from_mate[which].astype(F32) + (from_k, from_v)[which].astype(F32)
        base = lax.optimization_barrier(base)
        outs.append(base.at[ROWS - STRIPE :].add(total[0, which]))
    return grad_query, outs[0], outs[1]


def solution(mesh):
    spec = P(("parts", "ctx"), None)
    return jax.shard_map(
        body,
        mesh=mesh,
        in_specs=(spec,) * 5,
        out_specs=(spec,) * 3,
        check_vma=False,
    )
```

```python
import jax
import jax.numpy as jnp
from jax import lax
from jax.experimental import pallas as pl
from jax.experimental.pallas import tpu as pltpu
from jax.sharding import PartitionSpec as P

HEAD_DIM = 64
BLOCK = 128
WIN = 2
STRIPE = 16
NCOL = 16
LANES = 128
ROWS = WIN * BLOCK
EXT = 3 * ROWS
FAR = NCOL * STRIPE
SPAN = (2 * WIN + 1) * BLOCK
SCALE = HEAD_DIM**-0.5
NT = (((1,), (1,)), ((), ()))
BF16, F32 = jnp.bfloat16, jnp.float32


def tile(h, i):
    return slice((2 * h + i) * BLOCK, (2 * h + i + 1) * BLOCK)


def block_rows(i, flip):
    return pl.ds(pl.multiple_of((i ^ flip) * BLOCK, BLOCK), BLOCK)


def split_heads(ref, which, flip, two):
    first = lax.broadcasted_iota(jnp.int32, (BLOCK, LANES), 1) < HEAD_DIM
    for i in range(2):
        x = ref[which, block_rows(i, flip)]
        zero = jnp.zeros_like(x)
        two[tile(0, i)] = jnp.where(first, x, zero)
        two[tile(1, i)] = jnp.where(first, zero, x)


def both(i):
    return slice(2 * i * BLOCK, 2 * (i + 1) * BLOCK)


def stat(h, i):
    return tile(i, h)


def split_blocks(ref, which, flip, two):
    first = lax.broadcasted_iota(jnp.int32, (BLOCK, LANES), 1) < HEAD_DIM
    for i in range(2):
        x = ref[which, block_rows(i, flip)]
        zero = jnp.zeros_like(x)
        two[stat(0, i)] = jnp.where(first, x, zero)
        two[stat(1, i)] = jnp.where(first, zero, x)


def fill_window(flip, mate, own, which, across, ext):
    for i in range(2):
        rows = block_rows(i, flip)
        ext[tile(0, i)] = mate[rows]
        ext[tile(1, i)] = own[which, rows]
        ext[tile(2, i)] = across[rows]


def column_max(x):
    return jnp.max(x, axis=0, keepdims=True)


def column_sum(x):
    return jnp.sum(x, axis=0, keepdims=True)


def near_rows(i):
    return slice(i * BLOCK, i * BLOCK + SPAN)


def window_products(
    flags, biases, pair, own, mate_k, across_k, mate_v, across_v,
    near_s, near_d, stats,
    ext_k, ext_v, q_two, g_two,
):
    flip = flags[0]
    fill_window(flip, mate_k, own, 0, across_k, ext_k)
    fill_window(flip, mate_v, own, 1, across_v, ext_v)
    split_heads(pair, 0, flip, q_two)
    split_heads(pair, 1, flip, g_two)
    for h in range(2):
        heads = slice(h * ROWS, (h + 1) * ROWS)
        s = lax.dot_general(ext_k[...], q_two[heads], NT, preferred_element_type=F32)
        near_s[0, : 2 * ROWS, heads] = s[: 2 * ROWS]
        near_s[0, 2 * ROWS :, heads] = s[2 * ROWS :] + biases[0]
        near_d[0, :, heads] = lax.dot_general(
            ext_v[...], g_two[heads], NT, preferred_element_type=F32
        )


def window_stats(
    flags, biases, pair, own, mate_k, across_k, mate_v, across_v,
    near_s, near_d, stats,
    ext_k, ext_v, q_two, g_two,
):
    for h in range(2):
        for i in range(2):
            s = near_s[0, near_rows(i), tile(h, i)]
            d = near_d[0, near_rows(i), tile(h, i)]
            top = column_max(s)
            u = jnp.exp(s - top)
            stats[0, 0:1, stat(h, i)] = top
            stats[0, 1:2, stat(h, i)] = column_sum(u)
            stats[0, 2:3, stat(h, i)] = column_sum(u * d)


def stripe_products(
    flags, slots, pair, stats, table_a, table_b, table_c, table_d,
    coefs, far_query, keep_a, keep_b, send_a, send_b,
    far_k, far_v, q_two, g_two, far_s, far_d, far_probs, far_scores, table_sum, table,
):
    flip = flags[0]
    part = table_a.shape[0]
    for at, piece in enumerate((table_a, table_b, table_c, table_d)):
        table[at * part : (at + 1) * part] = piece[...]
    for i in range(2):
        for j in range(NCOL):
            slot = slots[0, i ^ flip, j]
            rows = slice(j * STRIPE, (j + 1) * STRIPE)
            for which, far in ((0, far_k), (1, far_v)):
                far[i, rows] = table[slot, which]
    split_blocks(pair, 0, flip, q_two)
    split_blocks(pair, 1, flip, g_two)
    for far, two, out in ((far_k, q_two, far_s), (far_v, g_two, far_d)):
        for i in range(2):
            out[:, both(i)] = lax.dot_general(
                far[i], two[both(i)], NT, preferred_element_type=F32
            )


def stripe_probs(
    flags, slots, pair, stats, table_a, table_b, table_c, table_d,
    coefs, far_query, keep_a, keep_b, send_a, send_b,
    far_k, far_v, q_two, g_two, far_s, far_d, far_probs, far_scores, table_sum, table,
):
    s, d = far_s[...], far_d[...]
    near_top = stats[0, 0:1]
    top = jnp.maximum(near_top, column_max(s))
    shrink = jnp.exp(near_top - top)
    u = jnp.exp(s - top)
    total = stats[0, 1:2] * shrink + column_sum(u)
    inv = 1.0 / total
    dot = (stats[0, 2:3] * shrink + column_sum(u * d)) * inv
    coefs[0, 0:1] = top + jnp.log(total)
    coefs[0, 1:2] = dot
    p = u * inv
    far_probs[...] = p.astype(BF16)
    far_scores[...] = (p * (d - dot)).astype(BF16)


def stripe_gradients(
    flags, slots, pair, stats, table_a, table_b, table_c, table_d,
    coefs, far_query, keep_a, keep_b, send_a, send_b,
    far_k, far_v, q_two, g_two, far_s, far_d, far_probs, far_scores, table_sum, table,
):
    flip = flags[0]
    part = table_a.shape[0]
    table_sum[...] = jnp.zeros_like(table_sum)
    for which, left, right in ((0, far_scores, q_two), (1, far_probs, g_two)):
        for i in range(2):
            far = jnp.dot(left[:, both(i)], right[both(i)], preferred_element_type=F32)
            parts = [far[j * STRIPE : (j + 1) * STRIPE] for j in range(NCOL)]
            places = [slots[1, i ^ flip, j] for j in range(NCOL)]
            if i == 1:
                parts = [x + table_sum[place, which] for x, place in zip(parts, places)]
            for x, place in zip(parts, places):
                table_sum[place, which] = x
    keep_a[...] = table_sum[:part]
    keep_b[...] = table_sum[part : 2 * part]
    send_a[...] = table_sum[2 * part : 3 * part].astype(send_a.dtype)
    send_b[...] = table_sum[3 * part :].astype(send_b.dtype)
    for i in range(2):
        out = jnp.dot(
            jnp.transpose(far_k[i]), far_scores[:, both(i)], preferred_element_type=F32
        )
        rows = slice(i * BLOCK, (i + 1) * BLOCK)
        far_query[0, :HEAD_DIM, rows] = out[:HEAD_DIM, :BLOCK]
        far_query[0, HEAD_DIM:, rows] = out[HEAD_DIM:, BLOCK:]


def window_probs(
    flags, pair, own, mate_k, across_k, near_s, near_d, coefs, far_query,
    grad_query, grad_key, grad_value, grad_mate, across_k_out, across_v_out,
    ext_k, q_two, g_two, probs, scores,
):
    flip = flags[0]
    fill_window(flip, mate_k, own, 0, across_k, ext_k)
    split_heads(pair, 0, flip, q_two)
    split_heads(pair, 1, flip, g_two)

    for h in range(2):
        for i in range(2):
            idle = slice((1 - i) * SPAN, (1 - i) * SPAN + BLOCK)
            probs[idle, tile(h, i)] = jnp.zeros((BLOCK, BLOCK), BF16)
            scores[idle, tile(h, i)] = jnp.zeros((BLOCK, BLOCK), BF16)

    for h in range(2):
        for i in range(2):
            rows = near_rows(i)
            p = jnp.exp(near_s[0, rows, tile(h, i)] - coefs[0, 0:1, stat(h, i)])
            probs[rows, tile(h, i)] = p.astype(BF16)
            ds = p * (near_d[0, rows, tile(h, i)] - coefs[0, 1:2, stat(h, i)])
            scores[rows, tile(h, i)] = ds.astype(BF16)


def window_gradients(
    flags, pair, own, mate_k, across_k, near_s, near_d, coefs, far_query,
    grad_query, grad_key, grad_value, grad_mate, across_k_out, across_v_out,
    ext_k, q_two, g_two, probs, scores,
):
    flip = flags[0]
    for which, left, right, grad_own, grad_across in (
        (1, probs, g_two, grad_value, across_v_out),
        (0, scores, q_two, grad_key, across_k_out),
    ):
        total = jnp.dot(left[...], right[...], preferred_element_type=F32)
        for i in range(2):
            rows = block_rows(i, flip)
            grad_mate[which, rows] = total[tile(0, i)].astype(grad_mate.dtype)
            grad_own[rows] = total[tile(1, i)]
            grad_across[rows] = total[tile(2, i)].astype(grad_across.dtype)
    k_t = jnp.transpose(ext_k[...])
    near = [
        jnp.dot(
            k_t[h * HEAD_DIM : (h + 1) * HEAD_DIM],
            scores[:, h * ROWS : (h + 1) * ROWS],
            preferred_element_type=F32,
        )
        for h in range(2)
    ]
    out = jnp.transpose(jnp.concatenate(near, axis=0) + far_query[0]) * SCALE
    for i in range(2):
        grad_query[block_rows(i, flip)] = out[i * BLOCK : (i + 1) * BLOCK]


SMEM_SPEC = pl.BlockSpec(memory_space=pltpu.SMEM)
VMEM_SPEC = pl.BlockSpec(memory_space=pltpu.VMEM)
TWO = pltpu.VMEM((2 * ROWS, LANES), BF16)
EXTENT = pltpu.VMEM((EXT, LANES), BF16)
FULL, ROW, PAIR, TABLE, STEP = "full", "row", "pair", "table", "step"


def view(ref, kind, p):
    lanes = pl.ds(p * LANES, LANES)
    if kind == ROW:
        return ref.at[:, lanes]
    if kind == PAIR:
        return ref.at[:, :, lanes]
    if kind == TABLE:
        return ref.at[:, :, :, lanes]
    if kind == STEP:
        return ref.at[pl.ds(p, 1)]
    return ref


def call(phases, steps, in_kinds, out_kinds, out_shape, scratch, flops, moved, args):
    kinds = in_kinds + out_kinds

    def whole(*refs):
        for phase in phases:
            for p in range(steps):
                views = [view(ref, kind, p) for ref, kind in zip(refs, kinds)]
                first = len(kinds) + p * len(scratch)
                phase(*views, *refs[first : first + len(scratch)])

    return pl.pallas_call(
        whole,
        in_specs=[SMEM_SPEC if kind == FULL else VMEM_SPEC for kind in in_kinds],
        out_specs=[VMEM_SPEC] * len(out_kinds),
        out_shape=[jax.ShapeDtypeStruct(shape, dtype) for shape, dtype in out_shape],
        scratch_shapes=scratch * steps,
        compiler_params=pltpu.CompilerParams(vmem_limit_bytes=32 << 20),
        cost_estimate=pl.CostEstimate(flops=flops, bytes_accessed=moved, transcendentals=1 << 20),
    )(*args)


def window_part(flags, biases, pair, own, mate_k, across_k, mate_v, across_v):
    steps = pair.shape[2] // LANES
    near = ((steps, EXT, 2 * ROWS), F32)
    return call(
        (window_products, window_stats),
        steps,
        [FULL, FULL, PAIR, PAIR, ROW, ROW, ROW, ROW],
        [STEP, STEP, STEP],
        [near, near, ((steps, 8, 2 * ROWS), F32)],
        [EXTENT, EXTENT, TWO, TWO],
        1 << 34,
        12 << 20,
        (flags, biases, pair, own, mate_k, across_k, mate_v, across_v),
    )


def stripe_part(flags, slots, pair, stats, *tables):
    part = tables[0].shape[0]
    width = pair.shape[2]
    steps = width // LANES
    return call(
        (stripe_products, stripe_probs, stripe_gradients),
        steps,
        [FULL, FULL, PAIR, STEP] + [TABLE] * 4,
        [STEP, STEP] + [TABLE] * 4,
        [((steps, 8, 2 * ROWS), F32), ((steps, LANES, ROWS), F32)]
        + [((part, 2, STRIPE, width), F32)] * 2
        + [((part, 2, STRIPE, width), BF16)] * 2,
        [
            pltpu.VMEM((2, FAR, LANES), BF16),
            pltpu.VMEM((2, FAR, LANES), BF16),
            TWO,
            TWO,
            pltpu.VMEM((FAR, 4 * BLOCK), F32),
            pltpu.VMEM((FAR, 4 * BLOCK), F32),
            pltpu.VMEM((FAR, 4 * BLOCK), BF16),
            pltpu.VMEM((FAR, 4 * BLOCK), BF16),
            pltpu.VMEM((4 * part, 2, STRIPE, LANES), F32),
            pltpu.VMEM((4 * part, 2, STRIPE, LANES), BF16),
        ],
        1 << 30,
        4 << 20,
        (flags, slots, pair, stats, *tables),
    )


def gradient_part(flags, pair, own, mate_k, across_k, near_s, near_d, coefs, far_query):
    width = pair.shape[2]
    steps = width // LANES
    return call(
        (window_probs, window_gradients),
        steps,
        [FULL, PAIR, PAIR, ROW, ROW, STEP, STEP, STEP, STEP],
        [ROW, ROW, ROW, PAIR, ROW, ROW],
        [((ROWS, width), F32)] * 3 + [((2, ROWS, width), BF16)] + [((ROWS, width), BF16)] * 2,
        [
            EXTENT,
            TWO,
            TWO,
            pltpu.VMEM((EXT, 2 * ROWS), BF16),
            pltpu.VMEM((EXT, 2 * ROWS), BF16),
        ],
        1 << 30,
        1 << 20,
        (flags, pair, own, mate_k, across_k, near_s, near_d, coefs, far_query),
    )


def stage_bits(count):
    bits = [1 << k for k in range(count.bit_length() - 1)]
    return bits[3:] + bits[2::-1]


def swapped(x, count, bit):
    return lax.ppermute(x, "ctx", [(i, i ^ bit) for i in range(count)])


def crossed(x, count):
    up = [(i, i + 1) for i in range(1, count - 1, 2)]
    return lax.ppermute(x, "ctx", up + [(j, i) for i, j in up])


def body(query_rows, key_rows, value_rows, grad_out, stripe_lists):
    count = lax.axis_size("ctx")
    me = lax.axis_index("ctx")
    bits = stage_bits(count)
    *z_bits, y_bit, x_bit, core_bit = bits
    relative = stripe_lists ^ me
    slots = jnp.stack(
        [
            sum(jnp.where((relative & bit) != 0, 1 << place, 0) for place, bit in enumerate(order))
            for order in ((*z_bits, y_bit, x_bit, core_bit), (*z_bits, x_bit, y_bit, core_bit))
        ]
    )
    flags = (1 - (me & 1)).reshape(1)
    alone = (me == 0) | (me == count - 1)
    biases = jnp.where(alone, -jnp.inf, 0.0).astype(F32).reshape(1)

    pair = jnp.stack([query_rows * BF16(SCALE), grad_out])
    own = jnp.stack([key_rows, value_rows])
    mate_k = swapped(key_rows, count, core_bit)
    mate_v = swapped(value_rows, count, core_bit)
    gathered = own[None, :, ROWS - STRIPE :]
    across_k = crossed(key_rows, count)
    for stage, bit in enumerate((*z_bits, y_bit)):
        if bit == y_bit:
            gathered, across_k = lax.optimization_barrier((gathered, across_k))
        gathered = jnp.concatenate([gathered, swapped(gathered, count, bit)], axis=0)
        if stage == 0:
            gathered, late = lax.optimization_barrier((gathered, value_rows))
            across_v = crossed(late, count)
    gathered, across_v = lax.optimization_barrier((gathered, across_v))
    near_s, near_d, stats = window_part(
        flags, biases, pair, own, mate_k, across_k, mate_v, across_v
    )
    beside = swapped(gathered, count, x_bit)
    beside, stats = lax.optimization_barrier((beside, stats))
    tables = [gathered, beside] + [swapped(x, count, core_bit) for x in (gathered, beside)]
    coefs, far_query, keep_a, keep_b, send_a, send_b = stripe_part(
        flags, slots, pair, stats, *tables
    )
    send = keep_b + swapped(send_b, count, core_bit).astype(F32)
    keep = keep_a + swapped(send_a, count, core_bit).astype(F32)
    send, coefs = lax.optimization_barrier((send.astype(BF16), coefs))
    grad_query, grad_key, grad_value, grad_mate, out_k, out_v = gradient_part(
        flags, pair, own, mate_k, across_k, near_s, near_d, coefs, far_query
    )
    from_v, from_k = crossed(out_v, count), crossed(out_k, count)
    total = keep + swapped(send, count, y_bit).astype(F32)
    total, grad_mate = lax.optimization_barrier((total, grad_mate))
    from_mate = swapped(grad_mate, count, core_bit)
    for bit in (x_bit, *z_bits[::-1]):
        half = total.shape[0] // 2
        keep, send = total[:half], total[half:].astype(BF16)
        if bit == z_bits[-1]:
            keep, from_v = lax.optimization_barrier((keep, from_v))
        if bit == z_bits[0]:
            keep, from_k = lax.optimization_barrier((keep, from_k))
        total = keep + swapped(send, count, bit).astype(F32)
    outs = []
    for which, grad_own in enumerate((grad_key, grad_value)):
        base = grad_own + from_mate[which].astype(F32) + (from_k, from_v)[which].astype(F32)
        base = lax.optimization_barrier(base)
        outs.append(base.at[ROWS - STRIPE :].add(total[0, which]))
    return grad_query, outs[0], outs[1]


def solution(mesh):
    spec = P(("parts", "ctx"), None)
    return jax.shard_map(
        body,
        mesh=mesh,
        in_specs=(spec,) * 5,
        out_specs=(spec,) * 3,
        check_vma=False,
    )
```

```python
import jax
import jax.numpy as jnp
from jax import lax
from jax.experimental import pallas as pl
from jax.experimental.pallas import tpu as pltpu
from jax.sharding import PartitionSpec as P

HEAD_DIM = 64
BLOCK = 128
WIN = 2
STRIPE = 16
NCOL = 16
LANES = 128
ROWS = WIN * BLOCK
EXT = 3 * ROWS
FAR = NCOL * STRIPE
SPAN = (2 * WIN + 1) * BLOCK
SCALE = HEAD_DIM**-0.5
NT = (((1,), (1,)), ((), ()))
BF16, F32 = jnp.bfloat16, jnp.float32


def tile(h, i):
    return slice((2 * h + i) * BLOCK, (2 * h + i + 1) * BLOCK)


def block_rows(i, flip):
    return pl.ds(pl.multiple_of((i ^ flip) * BLOCK, BLOCK), BLOCK)


def split_heads(ref, which, flip, two):
    first = lax.broadcasted_iota(jnp.int32, (BLOCK, LANES), 1) < HEAD_DIM
    for i in range(2):
        x = ref[which, block_rows(i, flip)]
        zero = jnp.zeros_like(x)
        two[tile(0, i)] = jnp.where(first, x, zero)
        two[tile(1, i)] = jnp.where(first, zero, x)


def both(i):
    return slice(2 * i * BLOCK, 2 * (i + 1) * BLOCK)


def stat(h, i):
    return tile(i, h)


def split_blocks(ref, which, flip, two):
    first = lax.broadcasted_iota(jnp.int32, (BLOCK, LANES), 1) < HEAD_DIM
    for i in range(2):
        x = ref[which, block_rows(i, flip)]
        zero = jnp.zeros_like(x)
        two[stat(0, i)] = jnp.where(first, x, zero)
        two[stat(1, i)] = jnp.where(first, zero, x)


def fill_window(flip, mate, own, which, across, ext):
    for i in range(2):
        rows = block_rows(i, flip)
        ext[tile(0, i)] = mate[rows]
        ext[tile(1, i)] = own[which, rows]
        ext[tile(2, i)] = across[rows]


def column_max(x):
    return jnp.max(x, axis=0, keepdims=True)


def column_sum(x):
    return jnp.sum(x, axis=0, keepdims=True)


def near_rows(i):
    return slice(i * BLOCK, i * BLOCK + SPAN)


def window_products(
    flags, biases, pair, own, mate_k, across_k, mate_v, across_v,
    near_s, near_d, stats,
    ext_k, ext_v, q_two, g_two,
):
    flip = flags[0]
    fill_window(flip, mate_k, own, 0, across_k, ext_k)
    fill_window(flip, mate_v, own, 1, across_v, ext_v)
    split_heads(pair, 0, flip, q_two)
    split_heads(pair, 1, flip, g_two)
    for h in range(2):
        heads = slice(h * ROWS, (h + 1) * ROWS)
        s = lax.dot_general(ext_k[...], q_two[heads], NT, preferred_element_type=F32)
        near_s[0, : 2 * ROWS, heads] = s[: 2 * ROWS]
        near_s[0, 2 * ROWS :, heads] = s[2 * ROWS :] + biases[0]
        near_d[0, :, heads] = lax.dot_general(
            ext_v[...], g_two[heads], NT, preferred_element_type=F32
        )


def window_stats(
    flags, biases, pair, own, mate_k, across_k, mate_v, across_v,
    near_s, near_d, stats,
    ext_k, ext_v, q_two, g_two,
):
    for h in range(2):
        for i in range(2):
            s = near_s[0, near_rows(i), tile(h, i)]
            d = near_d[0, near_rows(i), tile(h, i)]
            top = column_max(s)
            u = jnp.exp(s - top)
            stats[0, 0:1, stat(h, i)] = top
            stats[0, 1:2, stat(h, i)] = column_sum(u)
            stats[0, 2:3, stat(h, i)] = column_sum(u * d)


def stripe_products(
    flags, slots, pair, stats, table_a, table_b, table_c, table_d,
    coefs, far_k, far_scores, keep_a, keep_b, send_a, send_b,
    far_v, q_two, g_two, far_s, far_d, far_probs, table_sum, table,
):
    flip = flags[0]
    part = table_a.shape[0]
    for at, piece in enumerate((table_a, table_b, table_c, table_d)):
        table[at * part : (at + 1) * part] = piece[...]
    for i in range(2):
        for j in range(NCOL):
            slot = slots[0, i ^ flip, j]
            rows = slice(j * STRIPE, (j + 1) * STRIPE)
            for which, far in ((0, far_k.at[0]), (1, far_v)):
                far[i, rows] = table[slot, which]
    split_blocks(pair, 0, flip, q_two)
    split_blocks(pair, 1, flip, g_two)
    for far, two, out in ((far_k.at[0], q_two, far_s), (far_v, g_two, far_d)):
        for i in range(2):
            out[:, both(i)] = lax.dot_general(
                far[i], two[both(i)], NT, preferred_element_type=F32
            )


def stripe_probs(
    flags, slots, pair, stats, table_a, table_b, table_c, table_d,
    coefs, far_k, far_scores, keep_a, keep_b, send_a, send_b,
    far_v, q_two, g_two, far_s, far_d, far_probs, table_sum, table,
):
    s, d = far_s[...], far_d[...]
    near_top = stats[0, 0:1]
    top = jnp.maximum(near_top, column_max(s))
    shrink = jnp.exp(near_top - top)
    u = jnp.exp(s - top)
    total = stats[0, 1:2] * shrink + column_sum(u)
    inv = 1.0 / total
    dot = (stats[0, 2:3] * shrink + column_sum(u * d)) * inv
    coefs[0, 0:1] = top + jnp.log(total)
    coefs[0, 1:2] = dot
    p = u * inv
    far_probs[...] = p.astype(BF16)
    far_scores[0] = (p * (d - dot)).astype(BF16)


def stripe_gradients(
    flags, slots, pair, stats, table_a, table_b, table_c, table_d,
    coefs, far_k, far_scores, keep_a, keep_b, send_a, send_b,
    far_v, q_two, g_two, far_s, far_d, far_probs, table_sum, table,
):
    flip = flags[0]
    part = table_a.shape[0]
    table_sum[...] = jnp.zeros_like(table_sum)
    for which, left, right in ((0, far_scores.at[0], q_two), (1, far_probs, g_two)):
        for i in range(2):
            far = jnp.dot(left[:, both(i)], right[both(i)], preferred_element_type=F32)
            parts = [far[j * STRIPE : (j + 1) * STRIPE] for j in range(NCOL)]
            places = [slots[1, i ^ flip, j] for j in range(NCOL)]
            if i == 1:
                parts = [x + table_sum[place, which] for x, place in zip(parts, places)]
            for x, place in zip(parts, places):
                table_sum[place, which] = x
    keep_a[...] = table_sum[:part]
    keep_b[...] = table_sum[part : 2 * part]
    send_a[...] = table_sum[2 * part : 3 * part].astype(send_a.dtype)
    send_b[...] = table_sum[3 * part :].astype(send_b.dtype)


def window_probs(
    flags, pair, own, mate_k, across_k, near_s, near_d, coefs, far_k, far_scores,
    grad_query, grad_key, grad_value, grad_mate, across_k_out, across_v_out,
    ext_k, q_two, g_two, probs, scores,
):
    flip = flags[0]
    fill_window(flip, mate_k, own, 0, across_k, ext_k)
    split_heads(pair, 0, flip, q_two)
    split_heads(pair, 1, flip, g_two)

    for h in range(2):
        for i in range(2):
            idle = slice((1 - i) * SPAN, (1 - i) * SPAN + BLOCK)
            probs[idle, tile(h, i)] = jnp.zeros((BLOCK, BLOCK), BF16)
            scores[idle, tile(h, i)] = jnp.zeros((BLOCK, BLOCK), BF16)

    for h in range(2):
        for i in range(2):
            rows = near_rows(i)
            p = jnp.exp(near_s[0, rows, tile(h, i)] - coefs[0, 0:1, stat(h, i)])
            probs[rows, tile(h, i)] = p.astype(BF16)
            ds = p * (near_d[0, rows, tile(h, i)] - coefs[0, 1:2, stat(h, i)])
            scores[rows, tile(h, i)] = ds.astype(BF16)


def window_gradients(
    flags, pair, own, mate_k, across_k, near_s, near_d, coefs, far_k, far_scores,
    grad_query, grad_key, grad_value, grad_mate, across_k_out, across_v_out,
    ext_k, q_two, g_two, probs, scores,
):
    flip = flags[0]
    for which, left, right, grad_own, grad_across in (
        (1, probs, g_two, grad_value, across_v_out),
        (0, scores, q_two, grad_key, across_k_out),
    ):
        total = jnp.dot(left[...], right[...], preferred_element_type=F32)
        for i in range(2):
            rows = block_rows(i, flip)
            grad_mate[which, rows] = total[tile(0, i)].astype(grad_mate.dtype)
            grad_own[rows] = total[tile(1, i)]
            grad_across[rows] = total[tile(2, i)].astype(grad_across.dtype)
    k_t = jnp.transpose(ext_k[...])
    near = [
        jnp.dot(
            k_t[h * HEAD_DIM : (h + 1) * HEAD_DIM],
            scores[:, h * ROWS : (h + 1) * ROWS],
            preferred_element_type=F32,
        )
        for h in range(2)
    ]
    far = [
        jnp.dot(jnp.transpose(far_k[0, i]), far_scores[0, :, both(i)], preferred_element_type=F32)
        for i in range(2)
    ]
    far = [
        jnp.concatenate([x[:HEAD_DIM, :BLOCK], x[HEAD_DIM:, BLOCK:]], axis=0) for x in far
    ]
    out = jnp.transpose(jnp.concatenate(near, axis=0) + jnp.concatenate(far, axis=1)) * SCALE
    for i in range(2):
        grad_query[block_rows(i, flip)] = out[i * BLOCK : (i + 1) * BLOCK]


SMEM_SPEC = pl.BlockSpec(memory_space=pltpu.SMEM)
VMEM_SPEC = pl.BlockSpec(memory_space=pltpu.VMEM)
TWO = pltpu.VMEM((2 * ROWS, LANES), BF16)
EXTENT = pltpu.VMEM((EXT, LANES), BF16)
FULL, ROW, PAIR, TABLE, STEP = "full", "row", "pair", "table", "step"


def view(ref, kind, p):
    lanes = pl.ds(p * LANES, LANES)
    if kind == ROW:
        return ref.at[:, lanes]
    if kind == PAIR:
        return ref.at[:, :, lanes]
    if kind == TABLE:
        return ref.at[:, :, :, lanes]
    if kind == STEP:
        return ref.at[pl.ds(p, 1)]
    return ref


def call(phases, steps, in_kinds, out_kinds, out_shape, scratch, flops, moved, args):
    kinds = in_kinds + out_kinds

    def whole(*refs):
        for phase in phases:
            for p in range(steps):
                views = [view(ref, kind, p) for ref, kind in zip(refs, kinds)]
                first = len(kinds) + p * len(scratch)
                phase(*views, *refs[first : first + len(scratch)])

    return pl.pallas_call(
        whole,
        in_specs=[SMEM_SPEC if kind == FULL else VMEM_SPEC for kind in in_kinds],
        out_specs=[VMEM_SPEC] * len(out_kinds),
        out_shape=[jax.ShapeDtypeStruct(shape, dtype) for shape, dtype in out_shape],
        scratch_shapes=scratch * steps,
        compiler_params=pltpu.CompilerParams(vmem_limit_bytes=32 << 20),
        cost_estimate=pl.CostEstimate(flops=flops, bytes_accessed=moved, transcendentals=1 << 20),
    )(*args)


def window_part(flags, biases, pair, own, mate_k, across_k, mate_v, across_v):
    steps = pair.shape[2] // LANES
    near = ((steps, EXT, 2 * ROWS), F32)
    return call(
        (window_products, window_stats),
        steps,
        [FULL, FULL, PAIR, PAIR, ROW, ROW, ROW, ROW],
        [STEP, STEP, STEP],
        [near, near, ((steps, 8, 2 * ROWS), F32)],
        [EXTENT, EXTENT, TWO, TWO],
        1 << 34,
        12 << 20,
        (flags, biases, pair, own, mate_k, across_k, mate_v, across_v),
    )


def stripe_part(flags, slots, pair, stats, *tables):
    part = tables[0].shape[0]
    width = pair.shape[2]
    steps = width // LANES
    return call(
        (stripe_products, stripe_probs, stripe_gradients),
        steps,
        [FULL, FULL, PAIR, STEP] + [TABLE] * 4,
        [STEP, STEP, STEP] + [TABLE] * 4,
        [
            ((steps, 8, 2 * ROWS), F32),
            ((steps, 2, FAR, LANES), BF16),
            ((steps, FAR, 4 * BLOCK), BF16),
        ]
        + [((part, 2, STRIPE, width), F32)] * 2
        + [((part, 2, STRIPE, width), BF16)] * 2,
        [
            pltpu.VMEM((2, FAR, LANES), BF16),
            TWO,
            TWO,
            pltpu.VMEM((FAR, 4 * BLOCK), F32),
            pltpu.VMEM((FAR, 4 * BLOCK), F32),
            pltpu.VMEM((FAR, 4 * BLOCK), BF16),
            pltpu.VMEM((4 * part, 2, STRIPE, LANES), F32),
            pltpu.VMEM((4 * part, 2, STRIPE, LANES), BF16),
        ],
        1 << 30,
        4 << 20,
        (flags, slots, pair, stats, *tables),
    )


def gradient_part(flags, pair, own, mate_k, across_k, near_s, near_d, coefs, far_k, far_scores):
    width = pair.shape[2]
    steps = width // LANES
    return call(
        (window_probs, window_gradients),
        steps,
        [FULL, PAIR, PAIR, ROW, ROW, STEP, STEP, STEP, STEP, STEP],
        [ROW, ROW, ROW, PAIR, ROW, ROW],
        [((ROWS, width), F32)] * 3 + [((2, ROWS, width), BF16)] + [((ROWS, width), BF16)] * 2,
        [
            EXTENT,
            TWO,
            TWO,
            pltpu.VMEM((EXT, 2 * ROWS), BF16),
            pltpu.VMEM((EXT, 2 * ROWS), BF16),
        ],
        1 << 30,
        1 << 20,
        (flags, pair, own, mate_k, across_k, near_s, near_d, coefs, far_k, far_scores),
    )


def stage_bits(count):
    bits = [1 << k for k in range(count.bit_length() - 1)]
    return bits[3:] + bits[2::-1]


def swapped(x, count, bit):
    return lax.ppermute(x, "ctx", [(i, i ^ bit) for i in range(count)])


def crossed(x, count):
    up = [(i, i + 1) for i in range(1, count - 1, 2)]
    return lax.ppermute(x, "ctx", up + [(j, i) for i, j in up])


def body(query_rows, key_rows, value_rows, grad_out, stripe_lists):
    count = lax.axis_size("ctx")
    me = lax.axis_index("ctx")
    bits = stage_bits(count)
    *z_bits, y_bit, x_bit, core_bit = bits
    relative = stripe_lists ^ me
    slots = jnp.stack(
        [
            sum(jnp.where((relative & bit) != 0, 1 << place, 0) for place, bit in enumerate(order))
            for order in ((*z_bits, y_bit, x_bit, core_bit), (*z_bits, x_bit, y_bit, core_bit))
        ]
    )
    flags = (1 - (me & 1)).reshape(1)
    alone = (me == 0) | (me == count - 1)
    biases = jnp.where(alone, -jnp.inf, 0.0).astype(F32).reshape(1)

    pair = jnp.stack([query_rows * BF16(SCALE), grad_out])
    own = jnp.stack([key_rows, value_rows])
    mate_k = swapped(key_rows, count, core_bit)
    mate_v = swapped(value_rows, count, core_bit)
    gathered = own[None, :, ROWS - STRIPE :]
    across_k = crossed(key_rows, count)
    for stage, bit in enumerate((*z_bits, y_bit)):
        if bit == y_bit:
            gathered, across_k = lax.optimization_barrier((gathered, across_k))
        gathered = jnp.concatenate([gathered, swapped(gathered, count, bit)], axis=0)
        if stage == 0:
            gathered, late = lax.optimization_barrier((gathered, value_rows))
            across_v = crossed(late, count)
    gathered, across_v = lax.optimization_barrier((gathered, across_v))
    near_s, near_d, stats = window_part(
        flags, biases, pair, own, mate_k, across_k, mate_v, across_v
    )
    beside = swapped(gathered, count, x_bit)
    beside, stats = lax.optimization_barrier((beside, stats))
    tables = [gathered, beside] + [swapped(x, count, core_bit) for x in (gathered, beside)]
    coefs, far_k, far_scores, keep_a, keep_b, send_a, send_b = stripe_part(
        flags, slots, pair, stats, *tables
    )
    send = keep_b + swapped(send_b, count, core_bit).astype(F32)
    keep = keep_a + swapped(send_a, count, core_bit).astype(F32)
    send, coefs = lax.optimization_barrier((send.astype(BF16), coefs))
    grad_query, grad_key, grad_value, grad_mate, out_k, out_v = gradient_part(
        flags, pair, own, mate_k, across_k, near_s, near_d, coefs, far_k, far_scores
    )
    from_v, from_k = crossed(out_v, count), crossed(out_k, count)
    total = keep + swapped(send, count, y_bit).astype(F32)
    total, grad_mate = lax.optimization_barrier((total, grad_mate))
    from_mate = swapped(grad_mate, count, core_bit)
    for bit in (x_bit, *z_bits[::-1]):
        half = total.shape[0] // 2
        keep, send = total[:half], total[half:].astype(BF16)
        if bit == z_bits[-1]:
            keep, from_v = lax.optimization_barrier((keep, from_v))
        if bit == z_bits[0]:
            keep, from_k = lax.optimization_barrier((keep, from_k))
        total = keep + swapped(send, count, bit).astype(F32)
    outs = []
    for which, grad_own in enumerate((grad_key, grad_value)):
        base = grad_own + from_mate[which].astype(F32) + (from_k, from_v)[which].astype(F32)
        base = lax.optimization_barrier(base)
        outs.append(base.at[ROWS - STRIPE :].add(total[0, which]))
    return grad_query, outs[0], outs[1]


def solution(mesh):
    spec = P(("parts", "ctx"), None)
    return jax.shard_map(
        body,
        mesh=mesh,
        in_specs=(spec,) * 5,
        out_specs=(spec,) * 3,
        check_vma=False,
    )
```

```python
import jax
import jax.numpy as jnp
from jax import lax
from jax.experimental import pallas as pl
from jax.experimental.pallas import tpu as pltpu
from jax.sharding import PartitionSpec as P

HEAD_DIM = 64
BLOCK = 128
WIN = 2
STRIPE = 16
NCOL = 16
LANES = 128
ROWS = WIN * BLOCK
EXT = 3 * ROWS
FAR = NCOL * STRIPE
SPAN = (2 * WIN + 1) * BLOCK
SCALE = HEAD_DIM**-0.5
NT = (((1,), (1,)), ((), ()))
BF16, F32 = jnp.bfloat16, jnp.float32


def tile(h, i):
    return slice((2 * h + i) * BLOCK, (2 * h + i + 1) * BLOCK)


def block_rows(i, flip):
    return pl.ds(pl.multiple_of((i ^ flip) * BLOCK, BLOCK), BLOCK)


def split_heads(ref, which, flip, two):
    first = lax.broadcasted_iota(jnp.int32, (BLOCK, LANES), 1) < HEAD_DIM
    for i in range(2):
        x = ref[which, block_rows(i, flip)]
        zero = jnp.zeros_like(x)
        two[tile(0, i)] = jnp.where(first, x, zero)
        two[tile(1, i)] = jnp.where(first, zero, x)


def both(i):
    return slice(2 * i * BLOCK, 2 * (i + 1) * BLOCK)


def stat(h, i):
    return tile(i, h)


def split_blocks(ref, which, flip, two):
    first = lax.broadcasted_iota(jnp.int32, (BLOCK, LANES), 1) < HEAD_DIM
    for i in range(2):
        x = ref[which, block_rows(i, flip)]
        zero = jnp.zeros_like(x)
        two[stat(0, i)] = jnp.where(first, x, zero)
        two[stat(1, i)] = jnp.where(first, zero, x)


def fill_window(flip, mate, own, which, across, ext):
    for i in range(2):
        rows = block_rows(i, flip)
        ext[tile(0, i)] = mate[rows]
        ext[tile(1, i)] = own[which, rows]
        ext[tile(2, i)] = across[rows]


def column_max(x):
    return jnp.max(x, axis=0, keepdims=True)


def column_sum(x):
    return jnp.sum(x, axis=0, keepdims=True)


def near_rows(i):
    return slice(i * BLOCK, i * BLOCK + SPAN)


def window_products(
    flags, biases, pair, own, mate_k, across_k, mate_v, across_v,
    near_s, near_d, stats,
    ext_k, ext_v, q_two, g_two,
):
    flip = flags[0]
    fill_window(flip, mate_k, own, 0, across_k, ext_k)
    fill_window(flip, mate_v, own, 1, across_v, ext_v)
    split_heads(pair, 0, flip, q_two)
    split_heads(pair, 1, flip, g_two)
    for h in range(2):
        heads = slice(h * ROWS, (h + 1) * ROWS)
        s = lax.dot_general(ext_k[...], q_two[heads], NT, preferred_element_type=F32)
        near_s[0, : 2 * ROWS, heads] = s[: 2 * ROWS]
        near_s[0, 2 * ROWS :, heads] = s[2 * ROWS :] + biases[0]
        near_d[0, :, heads] = lax.dot_general(
            ext_v[...], g_two[heads], NT, preferred_element_type=F32
        )


def window_stats(
    flags, biases, pair, own, mate_k, across_k, mate_v, across_v,
    near_s, near_d, stats,
    ext_k, ext_v, q_two, g_two,
):
    for h in range(2):
        for i in range(2):
            s = near_s[0, near_rows(i), tile(h, i)]
            d = near_d[0, near_rows(i), tile(h, i)]
            top = column_max(s)
            u = jnp.exp(s - top)
            stats[0, 0:1, stat(h, i)] = top
            stats[0, 1:2, stat(h, i)] = column_sum(u)
            stats[0, 2:3, stat(h, i)] = column_sum(u * d)


def stripe_products(
    flags, slots, pair, stats, table_a, table_b, table_c, table_d,
    coefs, far_query, keep_a, keep_b, send_a, send_b,
    far_k, far_v, q_two, g_two, far_s, far_d, far_probs, far_scores, table_sum, table,
):
    flip = flags[0]
    part = table_a.shape[0]
    for at, piece in enumerate((table_a, table_b, table_c, table_d)):
        table[at * part : (at + 1) * part] = piece[...]
    for i in range(2):
        for j in range(NCOL):
            slot = slots[0, i ^ flip, j]
            rows = slice(j * STRIPE, (j + 1) * STRIPE)
            for which, far in ((0, far_k), (1, far_v)):
                far[i, rows] = table[slot, which]
    split_blocks(pair, 0, flip, q_two)
    split_blocks(pair, 1, flip, g_two)
    for far, two, out in ((far_k, q_two, far_s), (far_v, g_two, far_d)):
        for i in range(2):
            out[:, both(i)] = lax.dot_general(
                far[i], two[both(i)], NT, preferred_element_type=F32
            )


def stripe_probs(
    flags, slots, pair, stats, table_a, table_b, table_c, table_d,
    coefs, far_query, keep_a, keep_b, send_a, send_b,
    far_k, far_v, q_two, g_two, far_s, far_d, far_probs, far_scores, table_sum, table,
):
    s, d = far_s[...], far_d[...]
    near_top = stats[0, 0:1]
    top = jnp.maximum(near_top, column_max(s))
    shrink = jnp.exp(near_top - top)
    u = jnp.exp(s - top)
    total = stats[0, 1:2] * shrink + column_sum(u)
    inv = 1.0 / total
    dot = (stats[0, 2:3] * shrink + column_sum(u * d)) * inv
    coefs[0, 0:1] = top + jnp.log(total)
    coefs[0, 1:2] = dot
    p = u * inv
    far_probs[...] = p.astype(BF16)
    far_scores[...] = (p * (d - dot)).astype(BF16)


def stripe_gradients(
    flags, slots, pair, stats, table_a, table_b, table_c, table_d,
    coefs, far_query, keep_a, keep_b, send_a, send_b,
    far_k, far_v, q_two, g_two, far_s, far_d, far_probs, far_scores, table_sum, table,
):
    flip = flags[0]
    part = table_a.shape[0]
    table_sum[...] = jnp.zeros_like(table_sum)
    for which, left, right in ((0, far_scores, q_two), (1, far_probs, g_two)):
        for i in range(2):
            far = jnp.dot(left[:, both(i)], right[both(i)], preferred_element_type=F32)
            parts = [far[j * STRIPE : (j + 1) * STRIPE] for j in range(NCOL)]
            places = [slots[1, i ^ flip, j] for j in range(NCOL)]
            if i == 1:
                parts = [x + table_sum[place, which] for x, place in zip(parts, places)]
            for x, place in zip(parts, places):
                table_sum[place, which] = x
    keep_a[...] = table_sum[:part]
    keep_b[...] = table_sum[part : 2 * part]
    send_a[...] = table_sum[2 * part : 3 * part].astype(send_a.dtype)
    send_b[...] = table_sum[3 * part :].astype(send_b.dtype)
    for i in range(2):
        out = jnp.dot(
            jnp.transpose(far_k[i]), far_scores[:, both(i)], preferred_element_type=F32
        )
        rows = slice(i * BLOCK, (i + 1) * BLOCK)
        far_query[0, :HEAD_DIM, rows] = out[:HEAD_DIM, :BLOCK]
        far_query[0, HEAD_DIM:, rows] = out[HEAD_DIM:, BLOCK:]


def window_probs(
    flags, pair, own, mate_k, across_k, near_s, near_d, coefs, far_query,
    grad_query, grad_key, grad_value, grad_mate, across_k_out, across_v_out,
    ext_k, q_two, g_two, probs, scores,
):
    flip = flags[0]
    fill_window(flip, mate_k, own, 0, across_k, ext_k)
    split_heads(pair, 0, flip, q_two)
    split_heads(pair, 1, flip, g_two)

    for h in range(2):
        for i in range(2):
            idle = slice((1 - i) * SPAN, (1 - i) * SPAN + BLOCK)
            probs[idle, tile(h, i)] = jnp.zeros((BLOCK, BLOCK), BF16)
            scores[idle, tile(h, i)] = jnp.zeros((BLOCK, BLOCK), BF16)

    for h in range(2):
        for i in range(2):
            rows = near_rows(i)
            p = jnp.exp(near_s[0, rows, tile(h, i)] - coefs[0, 0:1, stat(h, i)])
            probs[rows, tile(h, i)] = p.astype(BF16)
            ds = p * (near_d[0, rows, tile(h, i)] - coefs[0, 1:2, stat(h, i)])
            scores[rows, tile(h, i)] = ds.astype(BF16)


def window_gradients(
    flags, pair, own, mate_k, across_k, near_s, near_d, coefs, far_query,
    grad_query, grad_key, grad_value, grad_mate, across_k_out, across_v_out,
    ext_k, q_two, g_two, probs, scores,
):
    flip = flags[0]
    for which, left, right, grad_own, grad_across in (
        (1, probs, g_two, grad_value, across_v_out),
        (0, scores, q_two, grad_key, across_k_out),
    ):
        total = jnp.dot(left[...], right[...], preferred_element_type=F32)
        for i in range(2):
            rows = block_rows(i, flip)
            grad_mate[which, rows] = total[tile(0, i)].astype(grad_mate.dtype)
            grad_own[rows] = total[tile(1, i)]
            grad_across[rows] = total[tile(2, i)].astype(grad_across.dtype)
    k_t = jnp.transpose(ext_k[...])
    near = [
        jnp.dot(
            k_t[h * HEAD_DIM : (h + 1) * HEAD_DIM],
            scores[:, h * ROWS : (h + 1) * ROWS],
            preferred_element_type=F32,
        )
        for h in range(2)
    ]
    out = jnp.transpose(jnp.concatenate(near, axis=0) + far_query[0]) * SCALE
    for i in range(2):
        grad_query[block_rows(i, flip)] = out[i * BLOCK : (i + 1) * BLOCK]


SMEM_SPEC = pl.BlockSpec(memory_space=pltpu.SMEM)
VMEM_SPEC = pl.BlockSpec(memory_space=pltpu.VMEM)
TWO = pltpu.VMEM((2 * ROWS, LANES), BF16)
EXTENT = pltpu.VMEM((EXT, LANES), BF16)
FULL, ROW, PAIR, TABLE, STEP = "full", "row", "pair", "table", "step"


def view(ref, kind, p):
    lanes = pl.ds(p * LANES, LANES)
    if kind == ROW:
        return ref.at[:, lanes]
    if kind == PAIR:
        return ref.at[:, :, lanes]
    if kind == TABLE:
        return ref.at[:, :, :, lanes]
    if kind == STEP:
        return ref.at[pl.ds(p, 1)]
    return ref


def call(phases, steps, in_kinds, out_kinds, out_shape, scratch, flops, moved, args):
    kinds = in_kinds + out_kinds

    def whole(*refs):
        for phase in phases:
            for p in range(steps):
                views = [view(ref, kind, p) for ref, kind in zip(refs, kinds)]
                first = len(kinds) + p * len(scratch)
                phase(*views, *refs[first : first + len(scratch)])

    return pl.pallas_call(
        whole,
        in_specs=[SMEM_SPEC if kind == FULL else VMEM_SPEC for kind in in_kinds],
        out_specs=[VMEM_SPEC] * len(out_kinds),
        out_shape=[jax.ShapeDtypeStruct(shape, dtype) for shape, dtype in out_shape],
        scratch_shapes=scratch * steps,
        compiler_params=pltpu.CompilerParams(vmem_limit_bytes=32 << 20),
        cost_estimate=pl.CostEstimate(flops=flops, bytes_accessed=moved, transcendentals=1 << 20),
    )(*args)


def window_part(flags, biases, pair, own, mate_k, across_k, mate_v, across_v):
    steps = pair.shape[2] // LANES
    near = ((steps, EXT, 2 * ROWS), F32)
    return call(
        (window_products, window_stats),
        steps,
        [FULL, FULL, PAIR, PAIR, ROW, ROW, ROW, ROW],
        [STEP, STEP, STEP],
        [near, near, ((steps, 8, 2 * ROWS), F32)],
        [EXTENT, EXTENT, TWO, TWO],
        1 << 34,
        12 << 20,
        (flags, biases, pair, own, mate_k, across_k, mate_v, across_v),
    )


def stripe_part(flags, slots, pair, stats, *tables):
    part = tables[0].shape[0]
    width = pair.shape[2]
    steps = width // LANES
    return call(
        (stripe_products, stripe_probs, stripe_gradients),
        steps,
        [FULL, FULL, PAIR, STEP] + [TABLE] * 4,
        [STEP, STEP] + [TABLE] * 4,
        [((steps, 8, 2 * ROWS), F32), ((steps, LANES, ROWS), F32)]
        + [((part, 2, STRIPE, width), F32)] * 2
        + [((part, 2, STRIPE, width), BF16)] * 2,
        [
            pltpu.VMEM((2, FAR, LANES), BF16),
            pltpu.VMEM((2, FAR, LANES), BF16),
            TWO,
            TWO,
            pltpu.VMEM((FAR, 4 * BLOCK), F32),
            pltpu.VMEM((FAR, 4 * BLOCK), F32),
            pltpu.VMEM((FAR, 4 * BLOCK), BF16),
            pltpu.VMEM((FAR, 4 * BLOCK), BF16),
            pltpu.VMEM((4 * part, 2, STRIPE, LANES), F32),
            pltpu.VMEM((4 * part, 2, STRIPE, LANES), BF16),
        ],
        1 << 30,
        4 << 20,
        (flags, slots, pair, stats, *tables),
    )


def gradient_part(flags, pair, own, mate_k, across_k, near_s, near_d, coefs, far_query):
    width = pair.shape[2]
    steps = width // LANES
    return call(
        (window_probs, window_gradients),
        steps,
        [FULL, PAIR, PAIR, ROW, ROW, STEP, STEP, STEP, STEP],
        [ROW, ROW, ROW, PAIR, ROW, ROW],
        [((ROWS, width), F32)] * 3 + [((2, ROWS, width), BF16)] + [((ROWS, width), BF16)] * 2,
        [
            EXTENT,
            TWO,
            TWO,
            pltpu.VMEM((EXT, 2 * ROWS), BF16),
            pltpu.VMEM((EXT, 2 * ROWS), BF16),
        ],
        1 << 30,
        1 << 20,
        (flags, pair, own, mate_k, across_k, near_s, near_d, coefs, far_query),
    )


def stage_bits(count):
    bits = [1 << k for k in range(count.bit_length() - 1)]
    return bits[3:] + bits[2::-1]


def swapped(x, count, bit):
    return lax.ppermute(x, "ctx", [(i, i ^ bit) for i in range(count)])


def crossed(x, count):
    up = [(i, i + 1) for i in range(1, count - 1, 2)]
    return lax.ppermute(x, "ctx", up + [(j, i) for i, j in up])


def body(query_rows, key_rows, value_rows, grad_out, stripe_lists):
    count = lax.axis_size("ctx")
    me = lax.axis_index("ctx")
    bits = stage_bits(count)
    *z_bits, y_bit, x_bit, core_bit = bits
    relative = stripe_lists ^ me
    slots = jnp.stack(
        [
            sum(jnp.where((relative & bit) != 0, 1 << place, 0) for place, bit in enumerate(order))
            for order in ((*z_bits, y_bit, x_bit, core_bit), (*z_bits, x_bit, y_bit, core_bit))
        ]
    )
    flags = (1 - (me & 1)).reshape(1)
    alone = (me == 0) | (me == count - 1)
    biases = jnp.where(alone, -jnp.inf, 0.0).astype(F32).reshape(1)

    pair = jnp.stack([query_rows * BF16(SCALE), grad_out])
    own = jnp.stack([key_rows, value_rows])
    mate_k = swapped(key_rows, count, core_bit)
    mate_v = swapped(value_rows, count, core_bit)
    gathered = own[None, :, ROWS - STRIPE :]
    across_k = crossed(key_rows, count)
    for stage, bit in enumerate((*z_bits, y_bit)):
        got = swapped(gathered, count, bit)
        if bit == y_bit:
            got, across_k = lax.optimization_barrier((got, across_k))
        gathered = jnp.concatenate([gathered, got], axis=0)
        if stage == 0:
            gathered, late = lax.optimization_barrier((gathered, value_rows))
            across_v = crossed(late, count)
    gathered, across_v = lax.optimization_barrier((gathered, across_v))
    near_s, near_d, stats = window_part(
        flags, biases, pair, own, mate_k, across_k, mate_v, across_v
    )
    beside = swapped(gathered, count, x_bit)
    beside, stats = lax.optimization_barrier((beside, stats))
    tables = [gathered, beside] + [swapped(x, count, core_bit) for x in (gathered, beside)]
    coefs, far_query, keep_a, keep_b, send_a, send_b = stripe_part(
        flags, slots, pair, stats, *tables
    )
    send = keep_b + swapped(send_b, count, core_bit).astype(F32)
    keep = keep_a + swapped(send_a, count, core_bit).astype(F32)
    send, coefs = lax.optimization_barrier((send.astype(BF16), coefs))
    grad_query, grad_key, grad_value, grad_mate, out_k, out_v = gradient_part(
        flags, pair, own, mate_k, across_k, near_s, near_d, coefs, far_query
    )
    from_v, from_k = crossed(out_v, count), crossed(out_k, count)
    total = keep + swapped(send, count, y_bit).astype(F32)
    total, grad_mate = lax.optimization_barrier((total, grad_mate))
    from_mate = swapped(grad_mate, count, core_bit)
    for bit in (x_bit, *z_bits[::-1]):
        half = total.shape[0] // 2
        keep, send = total[:half], total[half:].astype(BF16)
        if bit == z_bits[-1]:
            keep, from_v = lax.optimization_barrier((keep, from_v))
        if bit == z_bits[0]:
            keep, from_k = lax.optimization_barrier((keep, from_k))
        total = keep + swapped(send, count, bit).astype(F32)
    outs = []
    for which, grad_own in enumerate((grad_key, grad_value)):
        base = grad_own + from_mate[which].astype(F32) + (from_k, from_v)[which].astype(F32)
        base = lax.optimization_barrier(base)
        outs.append(base.at[ROWS - STRIPE :].add(total[0, which]))
    return grad_query, outs[0], outs[1]


def solution(mesh):
    spec = P(("parts", "ctx"), None)
    return jax.shard_map(
        body,
        mesh=mesh,
        in_specs=(spec,) * 5,
        out_specs=(spec,) * 3,
        check_vma=False,
    )
```
